256 devices in a mesh: pre: 16 (over x_lo, z), tp: 8 (over x_hi, y), dec: 2 (over core).
Axes of the slice: x: 4 (x_hi: 2, x_lo: 2; x = x_hi * 2 + x_lo), y: 4, z: 8, core: 2. Of those that a mesh axis runs over, the one named last changes fastest.
Arguments:
- tokens: bfloat16 [16384, 2048], P(('pre', 'tp', 'dec')), may hold values from -6 to 6
- route_ids: int32 [16384, 6], P(('pre', 'tp', 'dec')), may hold values from 0 to 63, all different within a row; in each aligned block of 64 rows (0 to 63, 64 to 127, ...) at most 12 rows name the same one
- route_weights: float32 [16384, 6], P(('pre', 'tp', 'dec')), may hold values from 0.05 to 0.4
- gate_weight: bfloat16 [2048, 90112], P(None, ('pre', 'tp')), may hold values from -0.125 to 0.125
- up_weight: bfloat16 [2048, 90112], P(None, ('pre', 'tp')), may hold values from -0.125 to 0.125
- down_weight: bfloat16 [90112, 2048], P(('pre', 'tp')), may hold values from -0.15625 to 0.15625
- prefill_cache: bfloat16 [2, 8, 256, 64, 1024], P(None, 'tp', 'pre', None, 'dec'), may hold values from -6 to 6
- handover_table: int32 [8, 256], replicated, may hold values from 0 to 255, as said below
Outputs:
- moe_output: bfloat16 [16384, 2048], P(('pre', 'tp', 'dec'))
- decode_cache: bfloat16 [2, 8, 256, 64, 1024], P(None, 'tp', 'pre', None, 'dec')
The draws below stay inside these ranges and needn't reach their ends.
Inputs may be any that keep to these rules, and one draw needn't show every extreme that they name: `route_ids`: each token names 6 different experts; within the rows of one device (64 consecutive tokens) no expert is named by more than 12 routes, a bound that some block reaches. `handover_table`: each row is a permutation of 0 to 255. The 16 slots g with g // 16 = s (one prefill device) map to at most 2 slots q with q // 16 = p (one decode device), for every s and p, and to exactly 2 for some pair.
All inputs are finite; a program needn't handle non-finite values.
Results may differ from the reference program's by a relative error of at most 0.0085.
Values may be sent and summed in bfloat16 or wider, within the bound.
No kernel may reach another device: no remote copies, remote signals or barrier semaphores. Data moves between devices by JAX's collectives and lax.ppermute only.
A program may use at most 128 MiB of HBM per device.

```python
import math
import jax
import jax.numpy as jnp
import numpy as np
from jax import lax

D = 2048
FF = 1408
TOPK = 6
TOK_DEV = 64
LAYERS = 2
BLK = 64
BLK_DEV = 16
EXPERTS = 64
TOKENS = 16384
MOST = 12
SOURCES = 16
COLUMNS = 8
POOL = 256
CW = 1024


def column_table(key):
    first, second, third = jax.random.split(key, 3)
    base = BLK_DEV // SOURCES
    quarter = max(1, SOURCES // 4)
    order = jax.random.permutation(first, SOURCES)
    place = jnp.zeros((SOURCES,), jnp.int32).at[order].set(jnp.arange(SOURCES, dtype=jnp.int32))
    raised = (place < quarter).astype(jnp.int32)
    lowered = ((place >= quarter) & (place < 2 * quarter)).astype(jnp.int32)
    counts = base + raised - lowered
    bounds = jnp.cumsum(counts)
    ranks = jnp.arange(BLK_DEV, dtype=jnp.int32)
    offset = jnp.sum((ranks[:, None] >= bounds[None, :]).astype(jnp.int32), axis=1)
    source_perm = jax.vmap(lambda item: jax.random.permutation(item, BLK_DEV))(jax.random.split(second, SOURCES))
    target_perm = jax.vmap(lambda item: jax.random.permutation(item, BLK_DEV))(jax.random.split(third, SOURCES))
    source_ids = jnp.arange(SOURCES, dtype=jnp.int32)[:, None]
    target_dev = (source_ids + offset[None, :]) % SOURCES
    target_slot = target_dev * BLK_DEV + target_perm[target_dev, ranks[None, :]]
    source_slot = source_ids * BLK_DEV + source_perm
    table = jnp.zeros((POOL,), jnp.int32).at[source_slot.reshape(-1)].set(target_slot.reshape(-1).astype(jnp.int32))
    return table


def draw_handover_table(key, part):
    keys = jax.random.split(jax.random.fold_in(key, 17), COLUMNS)
    return jax.vmap(column_table)(keys).astype(jnp.int32)


def block_levels(stream_key, extent, cuts, least, high):
    def one(dim, blocks):
        heights = jax.random.uniform(jax.random.fold_in(jax.random.fold_in(stream_key, 6), dim), (blocks,), jnp.float32, least / len(cuts), high / len(cuts))
        return jnp.repeat(jnp.exp(heights), extent[dim] // blocks).reshape((-1,) + (1,) * (len(extent) - dim - 1))

    level = one(*cuts[0])
    for cut in cuts[1:]:
        level = level * one(*cut)
    return level


def assign_block(stream_key, own, number, rows, amount, top, bound, lean):
    ranking = jax.random.permutation(stream_key, amount)
    crowded, common = load_shares(amount, rows * top, bound, lean, True), load_shares(amount, rows * top, bound, lean, False)
    places = jnp.arange(amount)

    def named(tallies, offset_by):
        used = int((tallies > 0).sum())
        fixed = max(1, used // 4)
        shifted = fixed + (places - fixed + offset_by * (used - fixed)) % max(1, amount - fixed)
        return jnp.zeros((amount,), jnp.int32).at[ranking[jnp.where(places < fixed, places, shifted)]].set(jnp.asarray(tallies, jnp.int32))

    tallies = jnp.where(number % 4 == 0, named(crowded, number // 4), named(common, number - number // 4 - 1))
    mixed = jax.random.permutation(jax.random.fold_in(own, 3), amount)
    donor, taker = mixed[0:amount // 2 * 2:2], mixed[1:amount // 2 * 2:2]
    room = jnp.minimum(tallies[donor] - 1, bound - tallies[taker]) // 2
    room = jnp.where((donor == ranking[0]) | (taker == ranking[0]) | (tallies[taker] == 0), 0, jnp.maximum(room, 0))
    shifted = jax.random.randint(jax.random.fold_in(own, 4), (amount // 2,), 0, 1 << 20) % (room + 1)
    tallies = tallies.at[donor].add(-shifted).at[taker].add(shifted)
    labels = jnp.searchsorted(jnp.cumsum(tallies), jnp.arange(rows * top), side="right").astype(jnp.int32)
    grid = labels.reshape(top, rows).T
    grid = grid[jax.random.permutation(jax.random.fold_in(own, 1), rows)]
    offset_by = jax.random.randint(jax.random.fold_in(own, 2), (rows, 1), 0, top)
    return jnp.take_along_axis(grid, (jnp.arange(top)[None, :] + offset_by) % top, axis=1)


def load_shares(amount, total, reach, skew, full):
    portions = [(1 << 20) // math.isqrt(rank ** skew) + 1 for rank in range(1, amount + 1)]
    largest = reach if full else min(reach, max(-(-total // amount), total * portions[0] // sum(portions)))
    least = 1 if total - largest >= amount - 1 else 0
    given, rest = [largest] + [least] * (amount - 1), total - largest - least * (amount - 1)
    while rest > 0:
        free = [i for i in range(1, amount) if given[i] < largest] or [i for i in range(1, amount) if given[i] < reach]
        pool, remaining = sum([portions[i] for i in free]), rest
        for i in free:
            more = min(reach - given[i], max(1, remaining * portions[i] // pool), rest)
            given[i] = given[i] + more
            rest = rest - more
    return np.array(given)


def gaussian(rng, dims, width, limit, shards=(), kind=jnp.bfloat16):
    level = block_levels(rng, dims, shards, -0.22, 0.18) if shards else 1.0
    array = jax.random.normal(rng, dims, jnp.float32) * width * level
    return jnp.minimum(jnp.maximum(array, -limit), limit).astype(kind)


def setup_inputs(seed: int = 0) -> dict:
    streams_of = jax.random.split(jax.random.key(seed), 9)
    tokens = gaussian(streams_of[0], (TOKENS, D), 1.0, 6.0, ((0, 256),))
    route_ids_keys = jax.random.split(jax.random.fold_in(streams_of[1], 1), TOKENS // TOK_DEV)
    route_ids_turns = jax.random.permutation(jax.random.fold_in(streams_of[1], 3), TOKENS // TOK_DEV)
    route_ids = jax.vmap(lambda own, number: assign_block(jax.random.fold_in(streams_of[1], 2), own, number, TOK_DEV, EXPERTS, TOPK, MOST, 2))(route_ids_keys, route_ids_turns).reshape((TOKENS, TOPK))
    route_weights = jnp.clip(0.05 + 0.35 * jax.random.uniform(streams_of[2], (TOKENS, TOPK), jnp.float32) ** block_levels(streams_of[2], (TOKENS, TOPK), ((0, 256),), -0.2, 0.2), 0.05, 0.4)
    gate_weight = gaussian(streams_of[3], (D, EXPERTS * FF), D ** -0.5, 0.125, ((1, 128),))
    up_weight = gaussian(streams_of[4], (D, EXPERTS * FF), D ** -0.5, 0.125, ((1, 128),))
    down_weight = gaussian(streams_of[5], (EXPERTS * FF, D), FF ** -0.5, 0.15625, ((0, 128),))
    prefill_cache = gaussian(streams_of[6], (LAYERS, COLUMNS, POOL, BLK, CW), 1.0, 6.0, ((1, 8), (2, 16), (4, 2)))
    handover_table = draw_handover_table(jax.random.fold_in(streams_of[8], 71), 0)
    return {"tokens": tokens, "route_ids": route_ids, "route_weights": route_weights, "gate_weight": gate_weight, "up_weight": up_weight, "down_weight": down_weight, "prefill_cache": prefill_cache, "handover_table": handover_table}


def reference(tokens, route_ids, route_weights, gate_weight, up_weight, down_weight, prefill_cache, handover_table):
    capacity = MOST * (TOKENS // TOK_DEV)
    ids_flat = route_ids.reshape(-1)
    weights_flat = route_weights.reshape(-1)
    token_of = (jnp.arange(TOKENS * TOPK, dtype=jnp.int32) // TOPK).astype(jnp.int32)

    def per_expert(total, expert):
        chosen = ids_flat == expert
        slot = jnp.cumsum(chosen.astype(jnp.int32)) - 1
        target = jnp.where(chosen, slot, capacity).astype(jnp.int32)
        rows = jnp.zeros((capacity,), jnp.int32).at[target].set(token_of, mode="drop")
        scale = jnp.zeros((capacity,), jnp.float32).at[target].set(weights_flat, mode="drop")
        inputs = tokens[rows]
        start = (expert * FF).astype(jnp.int32)
        gate_cols = lax.dynamic_slice_in_dim(gate_weight, start, FF, 1)
        up_cols = lax.dynamic_slice_in_dim(up_weight, start, FF, 1)
        down_rows = lax.dynamic_slice_in_dim(down_weight, start, FF, 0)
        gate = jnp.dot(inputs, gate_cols, preferred_element_type=jnp.float32)
        upper = jnp.dot(inputs, up_cols, preferred_element_type=jnp.float32)
        hidden = (jax.nn.silu(gate) * upper).astype(jnp.bfloat16)
        result = jnp.dot(hidden, down_rows, preferred_element_type=jnp.float32).astype(jnp.bfloat16)
        total = total.at[rows].add(scale[:, None] * result.astype(jnp.float32))
        return total, None

    start_total = jnp.zeros((TOKENS, D), jnp.float32)
    total, _ = lax.scan(per_expert, start_total, jnp.arange(EXPERTS, dtype=jnp.int32))
    moe_output = total.astype(jnp.bfloat16)

    columns = jnp.arange(COLUMNS, dtype=jnp.int32)[:, None]
    decode_cache = jnp.zeros_like(prefill_cache).at[:, columns, handover_table].set(prefill_cache)
    return moe_output, decode_cache
```

```python
import functools

import jax
import jax.numpy as jnp
from jax import lax
from jax.experimental import pallas as pl
from jax.experimental.pallas import tpu as pltpu
from jax.sharding import PartitionSpec as P

F32 = jnp.float32
BF16 = jnp.bfloat16
PARTS = 4


def iota(shape, dim):
    return lax.broadcasted_iota(jnp.int32, shape, dim)


def divide(x, by):
    return ((x.astype(F32) + 0.5) * (1.0 / by)).astype(jnp.int32)


def dot(a, b, contract):
    return lax.dot_general(a, b, (contract, ((), ())), preferred_element_type=F32)


def pick_mask(subrow, part_lane, slot, rows, chunk):
    group = divide(subrow, chunk)
    within = subrow - group * chunk
    part = divide(within, rows)
    row = within - part * rows
    place = (group & 1) * rows + row
    return (slot == place.astype(F32)) & (part == part_lane)


def pack_kernel(rows, ids_ref, w_ref, tok_ref, out_ref, slot_ref, whi_ref, wlo_ref, tok_sc):
    step = pl.program_id(0)
    count = ids_ref.shape[0]
    toks = ids_ref.shape[1]
    experts = slot_ref.shape[0]
    width = tok_ref.shape[1] // PARTS
    chunk = PARTS * rows

    @pl.when(step == 0)
    def _():
        eids = iota((experts, toks), 0)
        named = jnp.zeros((experts, toks), F32)
        weight = jnp.zeros((experts, toks), F32)
        for k in range(count):
            hit = ids_ref[k : k + 1, :] == eids
            named = named + jnp.where(hit, 1.0, 0.0)
            weight = weight + jnp.where(hit, w_ref[k : k + 1, :], 0.0)
        earlier = (iota((toks, toks), 0) < iota((toks, toks), 1)).astype(BF16)
        rank = dot(named.astype(BF16), earlier, ((1,), (0,)))
        slot = jnp.where(named > 0.5, rank, 255.0)
        high = weight.astype(BF16)
        low = (weight - high.astype(F32)).astype(BF16)
        slot_b = slot.astype(BF16)
        for p in range(PARTS):
            slot_ref[:, p * toks : (p + 1) * toks] = slot_b
            whi_ref[:, p * toks : (p + 1) * toks] = high
            wlo_ref[:, p * toks : (p + 1) * toks] = low
            tok_sc[p * toks : (p + 1) * toks, :] = tok_ref[:, p * width : (p + 1) * width]

    block = out_ref.shape[0]
    base = step * block
    subrow_e = base + iota((block, experts), 0)
    spread = (divide(subrow_e, 2 * chunk) == iota((block, experts), 1)).astype(BF16)
    slot_q = dot(spread, slot_ref[...], ((1,), (0,)))
    subrow = base + iota((block, PARTS * toks), 0)
    lane_part = divide(iota((block, PARTS * toks), 1), toks)
    mask = pick_mask(subrow, lane_part, slot_q, rows, chunk)
    out_ref[...] = dot(mask.astype(BF16), tok_sc[...], ((1,), (0,))).astype(BF16)


def pack(ids_t, w_t, tokens, experts, rows):
    toks, wide = tokens.shape
    chunk = PARTS * rows
    total = experts * 2 * chunk
    steps = 8
    width = wide // PARTS
    whole = lambda i: (0, 0)
    small = jax.ShapeDtypeStruct((experts, PARTS * toks), BF16)
    small_spec = pl.BlockSpec((experts, PARTS * toks), whole)

    return pl.pallas_call(
        functools.partial(pack_kernel, rows),
        grid=(steps,),
        in_specs=[
            pl.BlockSpec(ids_t.shape, whole),
            pl.BlockSpec(w_t.shape, whole),
            pl.BlockSpec(tokens.shape, whole),
        ],
        out_specs=[
            pl.BlockSpec((total // steps, width), lambda i: (i, 0)),
            small_spec,
            small_spec,
            small_spec,
        ],
        out_shape=[jax.ShapeDtypeStruct((total, width), BF16), small, small, small],
        scratch_shapes=[pltpu.VMEM((PARTS * toks, width), BF16)],
        name="pack",
    )(ids_t, w_t, tokens)


def combine_kernel(rows, slot_ref, whi_ref, wlo_ref, ret_ref, out_ref, acc):
    step = pl.program_id(0)
    experts, lanes = slot_ref.shape
    toks = lanes // PARTS
    block, width = ret_ref.shape
    chunk = PARTS * rows
    base = step * block
    subrow_e = base + iota((experts, block), 1)
    spread = (divide(subrow_e, 2 * chunk) == iota((experts, block), 0)).astype(BF16)
    slot_q = dot(slot_ref[...], spread, ((0,), (0,)))
    high = dot(whi_ref[...], spread, ((0,), (0,)))
    low = dot(wlo_ref[...], spread, ((0,), (0,)))
    subrow = base + iota((lanes, block), 1)
    lane_part = divide(iota((lanes, block), 0), toks)
    mask = pick_mask(subrow, lane_part, slot_q, rows, chunk)
    left = jnp.concatenate(
        [jnp.where(mask, high, 0.0).astype(BF16), jnp.where(mask, low, 0.0).astype(BF16)], axis=0
    )
    both = dot(left, ret_ref[...], ((1,), (0,)))
    part = both[:lanes] + both[lanes:]

    @pl.when(step == 0)
    def _():
        acc[...] = part

    @pl.when(step > 0)
    def _():
        acc[...] = acc[...] + part

    @pl.when(step == pl.num_programs(0) - 1)
    def _():
        for p in range(PARTS):
            out_ref[:, p * width : (p + 1) * width] = acc[p * toks : (p + 1) * toks, :].astype(BF16)


def combine(slot, whi, wlo, returned, rows):

    experts, lanes = slot.shape
    toks = lanes // PARTS
    total, width = returned.shape
    steps = 8
    whole = lambda i: (0, 0)
    return pl.pallas_call(
        functools.partial(combine_kernel, rows),
        grid=(steps,),
        in_specs=[
            pl.BlockSpec(slot.shape, whole),
            pl.BlockSpec(slot.shape, whole),
            pl.BlockSpec(slot.shape, whole),
            pl.BlockSpec((total // steps, width), lambda i: (i, 0)),
        ],
        out_specs=pl.BlockSpec((toks, PARTS * width), whole),
        out_shape=jax.ShapeDtypeStruct((toks, PARTS * width), BF16),
        scratch_shapes=[pltpu.VMEM((lanes, width), F32)],
        name="combine",
    )(slot, whi, wlo, returned)


def expert_kernel(
    rows, x_ref, g0, u0, d0, g1, u1, d1, g2, u2, d2, o_ref, wg, wu, wd, xs, acc, perm, sems
):
    half = g0.shape[0]
    quarter = g1.shape[0]
    copies = []
    for i, (src, dst, start) in enumerate(
        [
            (g0, wg, 0),
            (u0, wu, 0),
            (d0, wd, 0),
            (g1, wg, half),
            (u1, wu, half),
            (g2, wg, half + quarter),
            (u2, wu, half + quarter),
            (d1, wd, half),
            (d2, wd, half + quarter),
        ]
    ):
        copy = pltpu.make_async_copy(src, dst.at[pl.ds(start, src.shape[0])], sems.at[i])
        copy.start()
        copies.append(copy)

    sources = 16
    chunk = PARTS * rows
    small = sources * rows
    big = sources * chunk
    width = x_ref.shape[1]
    index = iota((big, big), 0)
    part = divide(index, small)
    rest = index - part * small
    source = divide(rest, rows)
    row = rest - source * rows
    perm[...] = (source * chunk + part * rows + row == iota((big, big), 1)).astype(BF16)

    def unpack(b, _):
        y = dot(perm[...], x_ref[pl.ds(b * big, big), :], ((1,), (0,))).astype(BF16)
        for p in range(PARTS):
            xs[pl.ds(b * small, small), p * width : (p + 1) * width] = y[
                p * small : (p + 1) * small, :
            ]
        return 0

    blocks = x_ref.shape[0] // big
    lax.fori_loop(0, blocks, unpack, 0)
    for copy in copies:
        copy.wait()

    total = wg.shape[0]
    cuts = list(range(0, total, 512)) + [total]
    mrows = 4 * small

    def run(m, _):
        x = xs[pl.ds(m * mrows, mrows), :]
        for c in range(len(cuts) - 1):
            lo, hi = cuts[c], cuts[c + 1]
            gate = dot(x, wg[lo:hi, :], ((1,), (1,)))
            upper = dot(x, wu[lo:hi, :], ((1,), (1,)))
            hidden = (gate / (1.0 + jnp.exp(-gate)) * upper).astype(BF16)
            res = dot(hidden, wd[lo:hi, :], ((1,), (0,)))
            if c == 0:
                acc[...] = res
            elif c < len(cuts) - 2:
                acc[...] = acc[...] + res
            else:
                xs[pl.ds(m * mrows, mrows), :] = (acc[...] + res).astype(BF16)
        return 0

    lax.fori_loop(0, xs.shape[0] // mrows, run, 0)

    def repack(b, _):
        y = jnp.concatenate(
            [
                xs[pl.ds(b * small, small), p * width : (p + 1) * width]
                for p in range(PARTS)
            ],
            axis=0,
        )
        o_ref[pl.ds(b * big, big), :] = dot(perm[...], y, ((0,), (0,))).astype(BF16)
        return 0

    lax.fori_loop(0, blocks, repack, 0)


def expert(x, own, first, second, rows):

    half, wide = own[0].shape
    total = 2 * half
    count = x.shape[0] // PARTS
    anyspec = pl.BlockSpec(memory_space=pl.ANY)
    vm = pl.BlockSpec(memory_space=pltpu.VMEM)
    big = 16 * PARTS * rows
    return pl.pallas_call(
        functools.partial(expert_kernel, rows),
        in_specs=[vm] + [anyspec] * 9,
        out_specs=vm,
        out_shape=jax.ShapeDtypeStruct(x.shape, BF16),
        scratch_shapes=[
            pltpu.VMEM((total, wide), BF16),
            pltpu.VMEM((total, wide), BF16),
            pltpu.VMEM((total, wide), BF16),
            pltpu.VMEM((count, wide), BF16),
            pltpu.VMEM((64 * rows, wide), F32),
            pltpu.VMEM((big, big), BF16),
            pltpu.SemaphoreType.DMA((9,)),
        ],
        compiler_params=pltpu.CompilerParams(vmem_limit_bytes=60 * 1024 * 1024),
        cost_estimate=pl.CostEstimate(
            flops=6 * count * total * wide,
            bytes_accessed=6 * total * wide + 2 * x.size * 2,
            transcendentals=count * total,
        ),
        name="expert",
    )(x, *own, *first, *second)


def copy_kernel(index_ref, in_ref, out_ref):
    out_ref[...] = in_ref[...].reshape(out_ref.shape)


def gather_out(index, cache):
    layers, blk_dev, blk, wide = cache.shape
    slots = index.shape[0]
    return pl.pallas_call(
        copy_kernel,
        grid_spec=pltpu.PrefetchScalarGridSpec(
            num_scalar_prefetch=1,
            grid=(slots,),
            in_specs=[pl.BlockSpec((layers, 1, blk, wide), lambda i, n: (0, n[i], 0, 0))],
            out_specs=pl.BlockSpec((1, layers, blk, wide), lambda i, n: (i, 0, 0, 0)),
        ),
        out_shape=jax.ShapeDtypeStruct((slots, layers, blk, wide), cache.dtype),
        name="gather_out",
    )(index, cache)


def gather_in(index, arrived):
    slots = index.shape[0]
    _, layers, blk, wide = arrived.shape
    return pl.pallas_call(
        copy_kernel,
        grid_spec=pltpu.PrefetchScalarGridSpec(
            num_scalar_prefetch=1,
            grid=(slots,),
            in_specs=[pl.BlockSpec((1, layers, blk, wide), lambda i, n: (n[i], 0, 0, 0))],
            out_specs=pl.BlockSpec((layers, 1, blk, wide), lambda i, n: (0, i, 0, 0)),
        ),
        out_shape=jax.ShapeDtypeStruct((layers, slots, blk, wide), arrived.dtype),
        name="gather_in",
    )(index, arrived)


def handover_indices(handover_table, sources, blk_dev, spare):
    column = lax.dynamic_index_in_dim(handover_table, lax.axis_index("tp"), 0, keepdims=False)
    here = lax.axis_index("pre")
    table = column.reshape(sources, blk_dev)
    dest = table // blk_dev
    earlier = jnp.arange(blk_dev)[:, None] < jnp.arange(blk_dev)[None, :]
    same = dest[:, :, None] == dest[:, None, :]
    rank = jnp.sum((same & earlier[None]).astype(jnp.int32), axis=1)
    my_dest = lax.dynamic_index_in_dim(dest, here, 0, keepdims=False)
    my_rank = lax.dynamic_index_in_dim(rank, here, 0, keepdims=False)
    wanted = jnp.arange(sources * spare, dtype=jnp.int32)
    out_index = jnp.sum(
        jnp.where(
            wanted[:, None] == (my_dest * spare + my_rank)[None, :],
            jnp.arange(blk_dev, dtype=jnp.int32)[None, :],
            0,
        ),
        axis=1,
    )
    place = here * blk_dev + jnp.arange(blk_dev, dtype=jnp.int32)
    came = jnp.arange(sources, dtype=jnp.int32)[:, None] * spare + rank
    in_index = jnp.sum(
        jnp.where(place[:, None, None] == table[None], came[None], 0), axis=(1, 2)
    )
    return out_index, in_index


def shards(
    tokens,
    route_ids,
    route_weights,
    gate_weight,
    up_weight,
    down_weight,
    prefill_cache,
    handover_table,
):
    tok_dev, wide = tokens.shape
    top_count = route_ids.shape[1]
    groups = lax.axis_size("pre") * lax.axis_size("tp")
    tp = lax.axis_size("tp")
    experts_all = groups // 2
    most = min(tok_dev, 2 * tok_dev * top_count // experts_all)
    rows = most // 2

    half = down_weight.shape[0]
    quarter = half // 2
    own = (gate_weight.T, up_weight.T, down_weight)
    core = lax.axis_index("dec")
    swap = [(i, i ^ 1) for i in range(tp)]
    first, second = [], []
    for weight in own:
        piece = lax.dynamic_slice_in_dim(weight, core * quarter, quarter, 0)
        got = lax.ppermute(piece, "tp", swap)
        first.append(got)
        second.append(lax.ppermute(got, "dec", [(0, 1), (1, 0)]))

    packed, slot, whi, wlo = pack(route_ids.T, route_weights.T, tokens, experts_all, rows)
    chunk = PARTS * rows
    width = wide // PARTS
    received = lax.all_to_all(
        packed.reshape(groups, chunk, width), ("pre", "tp"), split_axis=0, concat_axis=0, tiled=True
    )
    result = expert(received.reshape(groups * chunk, width), own, first, second, rows)
    returned = lax.all_to_all(
        result.reshape(groups, chunk, width), ("pre", "tp"), split_axis=0, concat_axis=0, tiled=True
    )
    moe_output = combine(slot, whi, wlo, returned.reshape(groups * chunk, width), rows)

    layers, _, blk_dev, blk, half_width = prefill_cache.shape
    sources = lax.axis_size("pre")
    spare = blk_dev // sources + 1
    out_index, in_index = handover_indices(handover_table, sources, blk_dev, spare)
    leaving = gather_out(out_index, prefill_cache[:, 0])
    arrived = lax.all_to_all(leaving, "pre", split_axis=0, concat_axis=0, tiled=True)
    decode_cache = gather_in(in_index, arrived)[:, None]
    return (moe_output, decode_cache)


def solution(mesh):
    return jax.shard_map(
        shards,
        mesh=mesh,
        in_specs=(
            P(("pre", "tp", "dec"), None),
            P(("pre", "tp", "dec"), None),
            P(("pre", "tp", "dec"), None),
            P(None, ("pre", "tp")),
            P(None, ("pre", "tp")),
            P(("pre", "tp"), None),
            P(None, "tp", "pre", None, "dec"),
            P(),
        ),
        out_specs=(P(("pre", "tp", "dec"), None), P(None, "tp", "pre", None, "dec")),
        check_vma=False,
    )
```

```python
import functools

import jax
import jax.numpy as jnp
from jax import lax
from jax.experimental import pallas as pl
from jax.experimental.pallas import tpu as pltpu
from jax.sharding import PartitionSpec as P


F32 = jnp.float32
BF16 = jnp.bfloat16
PARTS = 2


def iota(shape, dim):
    return lax.broadcasted_iota(jnp.int32, shape, dim)


def divide(x, by):
    return ((x.astype(F32) + 0.5) * (1.0 / by)).astype(jnp.int32)


def dot(a, b, contract):
    return lax.dot_general(a, b, (contract, ((), ())), preferred_element_type=F32)


def pick_mask(subrow, part_lane, slot, rows, chunk):
    within = subrow - divide(subrow, chunk) * chunk
    part = divide(within, rows)
    row = within - part * rows
    return (slot == row.astype(F32)) & (part == part_lane)


def pack_kernel(rows, ids_ref, w_ref, tok_ref, out_ref, slot_ref, whi_ref, wlo_ref, tok_sc):
    step = pl.program_id(0)
    count = ids_ref.shape[0]
    toks = ids_ref.shape[1]
    experts = slot_ref.shape[0]
    width = tok_ref.shape[1] // PARTS
    chunk = PARTS * rows

    @pl.when(step == 0)
    def _():
        eids = iota((experts, toks), 0)
        named = jnp.zeros((experts, toks), F32)
        weight = jnp.zeros((experts, toks), F32)
        for k in range(count):
            hit = ids_ref[k : k + 1, :] == eids
            named = named + jnp.where(hit, 1.0, 0.0)
            weight = weight + jnp.where(hit, w_ref[k : k + 1, :], 0.0)
        earlier = (iota((toks, toks), 0) < iota((toks, toks), 1)).astype(BF16)
        rank = dot(named.astype(BF16), earlier, ((1,), (0,)))
        slot = jnp.where(named > 0.5, rank, 255.0)
        high = weight.astype(BF16)
        low = (weight - high.astype(F32)).astype(BF16)
        slot_b = slot.astype(BF16)
        for p in range(PARTS):
            slot_ref[:, p * toks : (p + 1) * toks] = slot_b
            whi_ref[:, p * toks : (p + 1) * toks] = high
            wlo_ref[:, p * toks : (p + 1) * toks] = low
            tok_sc[p * toks : (p + 1) * toks, :] = tok_ref[:, p * width : (p + 1) * width]

    block = out_ref.shape[0]
    base = step * block
    subrow_e = base + iota((block, experts), 0)
    spread = (divide(subrow_e, chunk) == iota((block, experts), 1)).astype(BF16)
    slot_q = dot(spread, slot_ref[...], ((1,), (0,)))
    subrow = base + iota((block, PARTS * toks), 0)
    lane_part = divide(iota((block, PARTS * toks), 1), toks)
    mask = pick_mask(subrow, lane_part, slot_q, rows, chunk)
    out_ref[...] = dot(mask.astype(BF16), tok_sc[...], ((1,), (0,))).astype(BF16)


def pack(ids_t, w_t, tokens, experts, rows):
    toks, wide = tokens.shape
    chunk = PARTS * rows
    total = experts * chunk
    steps = 4
    width = wide // PARTS
    whole = lambda i: (0, 0)
    small = jax.ShapeDtypeStruct((experts, PARTS * toks), BF16)
    small_spec = pl.BlockSpec((experts, PARTS * toks), whole)

    return pl.pallas_call(
        functools.partial(pack_kernel, rows),
        grid=(steps,),
        in_specs=[
            pl.BlockSpec(ids_t.shape, whole),
            pl.BlockSpec(w_t.shape, whole),
            pl.BlockSpec(tokens.shape, whole),
        ],
        out_specs=[
            pl.BlockSpec((total // steps, width), lambda i: (i, 0)),
            small_spec,
            small_spec,
            small_spec,
        ],
        out_shape=[jax.ShapeDtypeStruct((total, width), BF16), small, small, small],
        scratch_shapes=[pltpu.VMEM((PARTS * toks, width), BF16)],
        name="pack",
    )(ids_t, w_t, tokens)


def combine_kernel(rows, slot_ref, whi_ref, wlo_ref, ret_ref, out_ref, acc):
    step = pl.program_id(0)
    experts, lanes = slot_ref.shape
    toks = lanes // PARTS
    block, width = ret_ref.shape
    chunk = PARTS * rows
    base = step * block
    subrow_e = base + iota((experts, block), 1)
    spread = (divide(subrow_e, chunk) == iota((experts, block), 0)).astype(BF16)
    slot_q = dot(slot_ref[...], spread, ((0,), (0,)))
    high = dot(whi_ref[...], spread, ((0,), (0,)))
    low = dot(wlo_ref[...], spread, ((0,), (0,)))
    subrow = base + iota((lanes, block), 1)
    lane_part = divide(iota((lanes, block), 0), toks)
    mask = pick_mask(subrow, lane_part, slot_q, rows, chunk)
    left = jnp.concatenate(
        [jnp.where(mask, high, 0.0).astype(BF16), jnp.where(mask, low, 0.0).astype(BF16)], axis=0
    )
    both = dot(left, ret_ref[...], ((1,), (0,)))
    part = both[:lanes] + both[lanes:]

    @pl.when(step == 0)
    def _():
        acc[...] = part

    @pl.when(step > 0)
    def _():
        acc[...] = acc[...] + part

    @pl.when(step == pl.num_programs(0) - 1)
    def _():
        for p in range(PARTS):
            out_ref[:, p * width : (p + 1) * width] = acc[p * toks : (p + 1) * toks, :].astype(BF16)


def combine(slot, whi, wlo, returned, rows):

    _, lanes = slot.shape
    toks = lanes // PARTS
    total, width = returned.shape
    steps = 4
    whole = lambda i: (0, 0)
    return pl.pallas_call(
        functools.partial(combine_kernel, rows),
        grid=(steps,),
        in_specs=[
            pl.BlockSpec(slot.shape, whole),
            pl.BlockSpec(slot.shape, whole),
            pl.BlockSpec(slot.shape, whole),
            pl.BlockSpec((total // steps, width), lambda i: (i, 0)),
        ],
        out_specs=pl.BlockSpec((toks, PARTS * width), whole),
        out_shape=jax.ShapeDtypeStruct((toks, PARTS * width), BF16),
        scratch_shapes=[pltpu.VMEM((lanes, width), F32)],
        name="combine",
    )(slot, whi, wlo, returned)


def expert_kernel(
    rows, x_ref, g0, u0, d0, g1, u1, d1, g2, u2, d2, o_ref, wg, wu, wd, xs, acc, perm, sems
):
    half = g0.shape[0]
    quarter = g1.shape[0]
    copies = []
    for i, (src, dst, start) in enumerate(
        [
            (g0, wg, 0),
            (u0, wu, 0),
            (d0, wd, 0),
            (g1, wg, half),
            (u1, wu, half),
            (g2, wg, half + quarter),
            (u2, wu, half + quarter),
            (d1, wd, half),
            (d2, wd, half + quarter),
        ]
    ):
        copy = pltpu.make_async_copy(src, dst.at[pl.ds(start, src.shape[0])], sems.at[i])
        copy.start()
        copies.append(copy)

    sources = 16
    chunk = PARTS * rows
    small = sources * rows
    big = sources * chunk
    width = x_ref.shape[1]
    index = iota((big, big), 0)
    part = divide(index, small)
    rest = index - part * small
    source = divide(rest, rows)
    row = rest - source * rows
    perm[...] = (source * chunk + part * rows + row == iota((big, big), 1)).astype(BF16)

    def unpack(b, _):
        y = dot(perm[...], x_ref[pl.ds(b * big, big), :], ((1,), (0,))).astype(BF16)
        for p in range(PARTS):
            xs[pl.ds(b * small, small), p * width : (p + 1) * width] = y[
                p * small : (p + 1) * small, :
            ]
        return 0

    blocks = x_ref.shape[0] // big
    lax.fori_loop(0, blocks, unpack, 0)
    for copy in copies:
        copy.wait()

    total = wg.shape[0]
    cuts = list(range(0, total, 512)) + [total]
    mrows = 2 * small

    def run(m, _):
        x = xs[pl.ds(m * mrows, mrows), :]
        for c in range(len(cuts) - 1):
            lo, hi = cuts[c], cuts[c + 1]
            gate = dot(x, wg[lo:hi, :], ((1,), (1,)))
            upper = dot(x, wu[lo:hi, :], ((1,), (1,)))
            hidden = (gate / (1.0 + jnp.exp(-gate)) * upper).astype(BF16)
            res = dot(hidden, wd[lo:hi, :], ((1,), (0,)))
            if c == 0:
                acc[...] = res
            elif c < len(cuts) - 2:
                acc[...] = acc[...] + res
            else:
                xs[pl.ds(m * mrows, mrows), :] = (acc[...] + res).astype(BF16)
        return 0

    lax.fori_loop(0, xs.shape[0] // mrows, run, 0)

    def repack(b, _):
        y = jnp.concatenate(
            [
                xs[pl.ds(b * small, small), p * width : (p + 1) * width]
                for p in range(PARTS)
            ],
            axis=0,
        )
        o_ref[pl.ds(b * big, big), :] = dot(perm[...], y, ((0,), (0,))).astype(BF16)
        return 0

    lax.fori_loop(0, blocks, repack, 0)


def expert(x, own, first, second, rows):

    half, wide = own[0].shape
    total = 2 * half
    count = x.shape[0] // PARTS
    anyspec = pl.BlockSpec(memory_space=pl.ANY)
    vm = pl.BlockSpec(memory_space=pltpu.VMEM)
    big = 16 * PARTS * rows
    return pl.pallas_call(
        functools.partial(expert_kernel, rows),
        in_specs=[vm] + [anyspec] * 9,
        out_specs=vm,
        out_shape=jax.ShapeDtypeStruct(x.shape, BF16),
        scratch_shapes=[
            pltpu.VMEM((total, wide), BF16),
            pltpu.VMEM((total, wide), BF16),
            pltpu.VMEM((total, wide), BF16),
            pltpu.VMEM((count, wide), BF16),
            pltpu.VMEM((32 * rows, wide), F32),
            pltpu.VMEM((big, big), BF16),
            pltpu.SemaphoreType.DMA((9,)),
        ],
        compiler_params=pltpu.CompilerParams(vmem_limit_bytes=60 * 1024 * 1024),
        cost_estimate=pl.CostEstimate(
            flops=6 * count * total * wide,
            bytes_accessed=6 * total * wide + 2 * x.size * 2,
            transcendentals=count * total,
        ),
        name="expert",
    )(x, *own, *first, *second)


def copy_kernel(index_ref, in_ref, out_ref):
    out_ref[...] = in_ref[...].reshape(out_ref.shape)


def gather_out(index, cache):
    layers, _, blk, wide = cache.shape
    slots = index.shape[0]
    return pl.pallas_call(
        copy_kernel,
        grid_spec=pltpu.PrefetchScalarGridSpec(
            num_scalar_prefetch=1,
            grid=(slots,),
            in_specs=[pl.BlockSpec((layers, 1, blk, wide), lambda i, n: (0, n[i], 0, 0))],
            out_specs=pl.BlockSpec((1, layers, blk, wide), lambda i, n: (i, 0, 0, 0)),
        ),
        out_shape=jax.ShapeDtypeStruct((slots, layers, blk, wide), cache.dtype),
        name="gather_out",
    )(index, cache)


def gather_in(index, arrived):
    slots = index.shape[0]
    _, layers, blk, wide = arrived.shape
    return pl.pallas_call(
        copy_kernel,
        grid_spec=pltpu.PrefetchScalarGridSpec(
            num_scalar_prefetch=1,
            grid=(slots,),
            in_specs=[pl.BlockSpec((1, layers, blk, wide), lambda i, n: (n[i], 0, 0, 0))],
            out_specs=pl.BlockSpec((layers, 1, blk, wide), lambda i, n: (0, i, 0, 0)),
        ),
        out_shape=jax.ShapeDtypeStruct((layers, slots, blk, wide), arrived.dtype),
        name="gather_in",
    )(index, arrived)


def handover_indices(handover_table, sources, blk_dev, spare):
    column = lax.dynamic_index_in_dim(handover_table, lax.axis_index("tp"), 0, keepdims=False)
    here = lax.axis_index("pre")
    table = column.reshape(sources, blk_dev)
    dest = table // blk_dev
    earlier = jnp.arange(blk_dev)[:, None] < jnp.arange(blk_dev)[None, :]
    same = dest[:, :, None] == dest[:, None, :]
    rank = jnp.sum((same & earlier[None]).astype(jnp.int32), axis=1)
    my_dest = lax.dynamic_index_in_dim(dest, here, 0, keepdims=False)
    my_rank = lax.dynamic_index_in_dim(rank, here, 0, keepdims=False)
    wanted = jnp.arange(sources * spare, dtype=jnp.int32)
    out_index = jnp.sum(
        jnp.where(
            wanted[:, None] == (my_dest * spare + my_rank)[None, :],
            jnp.arange(blk_dev, dtype=jnp.int32)[None, :],
            0,
        ),
        axis=1,
    )
    place = here * blk_dev + jnp.arange(blk_dev, dtype=jnp.int32)
    came = jnp.arange(sources, dtype=jnp.int32)[:, None] * spare + rank
    in_index = jnp.sum(
        jnp.where(place[:, None, None] == table[None], came[None], 0), axis=(1, 2)
    )
    return out_index, in_index


def shards(
    tokens,
    route_ids,
    route_weights,
    gate_weight,
    up_weight,
    down_weight,
    prefill_cache,
    handover_table,
):
    tok_dev, wide = tokens.shape
    top_count = route_ids.shape[1]
    tp = lax.axis_size("tp")
    groups = lax.axis_size("pre") * tp
    experts_all = groups // 2
    rows = min(tok_dev, 2 * tok_dev * top_count // experts_all)

    half = down_weight.shape[0]
    quarter = half // 2
    core = lax.axis_index("dec")
    swap = [(i, i ^ 1) for i in range(tp)]
    first, second = [], []
    own = (gate_weight.T, up_weight.T, down_weight)
    for weight in own:
        piece = lax.dynamic_slice_in_dim(weight, core * quarter, quarter, 0)
        got = lax.ppermute(piece, "tp", swap)
        first.append(got)
        second.append(lax.ppermute(got, "dec", [(0, 1), (1, 0)]))

    kinds = [[g for g in range(groups) if (g ^ (g >> 1)) & 1 == kind] for kind in (0, 1)]
    chunk = PARTS * rows
    width = wide // PARTS

    def exchange(rows_out):
        moved = lax.all_to_all(
            rows_out.reshape(experts_all, chunk, width),
            ("pre", "tp"),
            split_axis=0,
            concat_axis=0,
            axis_index_groups=kinds,
            tiled=True,
        )
        return moved.reshape(experts_all * chunk, width)

    packed, slot, whi, wlo = pack(route_ids.T, route_weights.T, tokens, experts_all, rows)
    received = exchange(packed)
    result = expert(received, own, first, second, rows)
    returned = exchange(result)
    moe_output = combine(slot, whi, wlo, returned, rows)

    _, _, blk_dev, _, _ = prefill_cache.shape
    sources = lax.axis_size("pre")
    spare = blk_dev // sources + 1
    out_index, in_index = handover_indices(handover_table, sources, blk_dev, spare)
    leaving = gather_out(out_index, prefill_cache[:, 0])
    arrived = lax.all_to_all(leaving, "pre", split_axis=0, concat_axis=0, tiled=True)
    decode_cache = gather_in(in_index, arrived)[:, None]
    return (moe_output, decode_cache)


def solution(mesh):
    return jax.shard_map(
        shards,
        mesh=mesh,
        in_specs=(
            P(("pre", "tp", "dec"), None),
            P(("pre", "tp", "dec"), None),
            P(("pre", "tp", "dec"), None),
            P(None, ("pre", "tp")),
            P(None, ("pre", "tp")),
            P(("pre", "tp"), None),
            P(None, "tp", "pre", None, "dec"),
            P(),
        ),
        out_specs=(P(("pre", "tp", "dec"), None), P(None, "tp", "pre", None, "dec")),
        check_vma=False,
    )
```

```python
import functools

import jax
import jax.numpy as jnp
from jax import lax
from jax.experimental import pallas as pl
from jax.experimental.pallas import tpu as pltpu
from jax.sharding import PartitionSpec as P


F32 = jnp.float32
BF16 = jnp.bfloat16
TOP = 6
ZS = 8
PEERS = 8
OFFSETS = (0, 1, 2, 3, 4, -1, -2, -3)


def iota(shape, dim):
    return lax.broadcasted_iota(jnp.int32, shape, dim)


def divide(x, by):
    return ((x.astype(F32) + 0.5) * (1.0 / by)).astype(jnp.int32)


def dot(a, b, contract):
    return lax.dot_general(a, b, (contract, ((), ())), preferred_element_type=F32)


def pick_mask(subrow, part_lane, slot, rows, chunk):
    within = subrow - divide(subrow, chunk) * chunk
    part = divide(within, rows)
    row = within - part * rows
    return (slot == row.astype(F32)) & (part == part_lane)


def pack_kernel(rows, parts, place_ref, *refs):
    blocks = refs[:ZS]
    outs = refs[ZS:]
    toks = blocks[0].shape[0]
    width = outs[0].shape[2]
    wide = width * parts
    chunk = parts * rows
    experts = toks
    me, z = place_ref[0], place_ref[1]
    peers = len(outs)

    def expert_of(index):
        peer = divide(index, chunk) ^ me
        return (peer >> 2) * 32 + z * 4 + (peer & 3)

    total = peers * chunk
    spread = (expert_of(iota((total, experts), 0)) == iota((total, experts), 1)).astype(BF16)
    earlier = (iota((toks, toks), 1) < iota((toks, toks), 0)).astype(BF16)
    index = iota((total, parts * toks), 0)
    lane_part = divide(iota((total, parts * toks), 1), toks)
    eids = iota((toks, experts), 1).astype(F32)
    for o, block in enumerate(blocks):
        ids = block[:, wide : wide + 128].astype(F32)
        named = jnp.zeros((toks, experts), F32)
        for k in range(TOP):
            named = named + jnp.where(ids[:, k : k + 1] == eids, 1.0, 0.0)
        rank = dot(earlier, named.astype(BF16), ((1,), (0,)))
        slot = jnp.where(named > 0.5, rank, 255.0).astype(BF16)
        slot = jnp.concatenate([slot] * parts, axis=0)
        slot_q = dot(spread, slot, ((1,), (1,)))
        mask = pick_mask(index, lane_part, slot_q, rows, chunk)
        source = jnp.concatenate(
            [block[:, p * width : (p + 1) * width] for p in range(parts)], axis=0
        )
        y = dot(mask.astype(BF16), source, ((1,), (0,)))
        for m, out in enumerate(outs):
            out[o] = y[m * chunk : (m + 1) * chunk, :].astype(BF16)


def pack(place, blocks, wide, rows, parts):
    shape = jax.ShapeDtypeStruct((ZS, parts * rows, wide // parts), BF16)
    vm = pl.BlockSpec(memory_space=pltpu.VMEM)
    return pl.pallas_call(
        functools.partial(pack_kernel, rows, parts),
        in_specs=[pl.BlockSpec(memory_space=pltpu.SMEM)] + [vm] * ZS,
        out_specs=[vm] * PEERS,
        out_shape=[shape] * PEERS,
        name="pack",
    )(place, *blocks)


def combine_kernel(rows, parts, ids_ref, w_ref, ret_ref, out_ref, slot_ref, whi_ref, wlo_ref, acc):
    step = pl.program_id(0)
    count, toks = ids_ref.shape
    experts, lanes = slot_ref.shape
    block, width = ret_ref.shape
    chunk = parts * rows

    @pl.when(step == 0)
    def _():
        eids = iota((experts, toks), 0)
        named = jnp.zeros((experts, toks), F32)
        weight = jnp.zeros((experts, toks), F32)
        for k in range(count):
            hit = ids_ref[k : k + 1, :] == eids
            named = named + jnp.where(hit, 1.0, 0.0)
            weight = weight + jnp.where(hit, w_ref[k : k + 1, :], 0.0)
        earlier = (iota((toks, toks), 0) < iota((toks, toks), 1)).astype(BF16)
        rank = dot(named.astype(BF16), earlier, ((1,), (0,)))
        slot = jnp.where(named > 0.5, rank, 255.0).astype(BF16)
        high = weight.astype(BF16)
        low = (weight - high.astype(F32)).astype(BF16)
        for p in range(parts):
            slot_ref[:, p * toks : (p + 1) * toks] = slot
            whi_ref[:, p * toks : (p + 1) * toks] = high
            wlo_ref[:, p * toks : (p + 1) * toks] = low

    base = step * block
    subrow_e = base + iota((experts, block), 1)
    spread = (divide(subrow_e, chunk) == iota((experts, block), 0)).astype(BF16)
    slot_q = dot(slot_ref[...], spread, ((0,), (0,)))
    high = dot(whi_ref[...], spread, ((0,), (0,)))
    low = dot(wlo_ref[...], spread, ((0,), (0,)))
    subrow = base + iota((lanes, block), 1)
    lane_part = divide(iota((lanes, block), 0), toks)
    mask = pick_mask(subrow, lane_part, slot_q, rows, chunk)
    left = jnp.concatenate(
        [jnp.where(mask, high, 0.0).astype(BF16), jnp.where(mask, low, 0.0).astype(BF16)], axis=0
    )
    both = dot(left, ret_ref[...], ((1,), (0,)))
    part = both[:lanes] + both[lanes:]

    @pl.when(step == 0)
    def _():
        acc[...] = part

    @pl.when(step > 0)
    def _():
        acc[...] = acc[...] + part

    @pl.when(step == pl.num_programs(0) - 1)
    def _():
        for p in range(parts):
            out_ref[:, p * width : (p + 1) * width] = acc[p * toks : (p + 1) * toks, :].astype(BF16)


def combine(ids_t, w_t, returned, experts, rows, parts):
    toks = ids_t.shape[1]
    lanes = parts * toks
    total, width = returned.shape
    steps = 4
    whole = lambda i: (0, 0)
    return pl.pallas_call(
        functools.partial(combine_kernel, rows, parts),
        grid=(steps,),
        in_specs=[
            pl.BlockSpec(ids_t.shape, whole),
            pl.BlockSpec(w_t.shape, whole),
            pl.BlockSpec((total // steps, width), lambda i: (i, 0)),
        ],
        out_specs=pl.BlockSpec((toks, parts * width), whole),
        out_shape=jax.ShapeDtypeStruct((toks, parts * width), BF16),
        scratch_shapes=[pltpu.VMEM((experts, lanes), BF16)] * 3 + [pltpu.VMEM((lanes, width), F32)],
        name="combine",
    )(ids_t, w_t, returned)


def permutation(size, items, parts, rows):
    small = items * rows
    index = iota((size, size), 0)
    part = divide(index, small)
    rest = index - part * small
    item = divide(rest, rows)
    row = rest - item * rows
    return (item * (parts * rows) + part * rows + row == iota((size, size), 1)).astype(BF16)


def expert_kernel(rows, parts, back, place_ref, *refs):
    xin = refs[:PEERS]
    g0, u0, d0, g1, u1, d1, g2, u2, d2 = refs[PEERS : PEERS + 9]
    o_ref, wg, wu, wd, xs, acc, perm, perm_back, sems = refs[PEERS + 9 :]
    half = g0.shape[0]
    quarter = g1.shape[0]
    copies = []
    for i, (src, dst, start) in enumerate(
        [
            (g0, wg, 0),
            (u0, wu, 0),
            (d0, wd, 0),
            (g1, wg, half),
            (u1, wu, half),
            (g2, wg, half + quarter),
            (u2, wu, half + quarter),
            (d1, wd, half),
            (d2, wd, half + quarter),
        ]
    ):
        copy = pltpu.make_async_copy(src, dst.at[pl.ds(start, src.shape[0])], sems.at[i])
        copy.start()
        copies.append(copy)

    small = ZS * rows
    wide = xs.shape[1]
    width = wide // parts
    perm[...] = permutation(parts * small, ZS, parts, rows)
    perm_back[...] = permutation(back * small, ZS, back, rows)
    for m in range(PEERS):
        y = dot(perm[...], xin[m][...], ((1,), (0,))).astype(BF16)
        for p in range(parts):
            xs[m * small : (m + 1) * small, p * width : (p + 1) * width] = y[
                p * small : (p + 1) * small, :
            ]
    for copy in copies:
        copy.wait()

    total = wg.shape[0]
    cuts = list(range(0, total, 512)) + [total]
    mrows = acc.shape[0]

    def run(m, _):
        x = xs[pl.ds(m * mrows, mrows), :]
        for c in range(len(cuts) - 1):
            lo, hi = cuts[c], cuts[c + 1]
            gate = dot(x, wg[lo:hi, :], ((1,), (1,)))
            upper = dot(x, wu[lo:hi, :], ((1,), (1,)))
            hidden = (gate / (1.0 + jnp.exp(-gate)) * upper).astype(BF16)
            res = dot(hidden, wd[lo:hi, :], ((1,), (0,)))
            if c == 0:
                acc[...] = res
            elif c < len(cuts) - 2:
                acc[...] = acc[...] + res
            else:
                xs[pl.ds(m * mrows, mrows), :] = (acc[...] + res).astype(BF16)
        return 0

    lax.fori_loop(0, xs.shape[0] // mrows, run, 0)

    me, z = place_ref[0], place_ref[1]
    width = wide // back
    chunk = back * rows
    for m in range(PEERS):
        y = jnp.concatenate(
            [
                xs[m * small : (m + 1) * small, p * width : (p + 1) * width]
                for p in range(back)
            ],
            axis=0,
        )
        y = dot(perm_back[...], y, ((0,), (0,)))
        peer = me ^ m
        for o in range(ZS):
            home = (peer >> 2) * 32 + ((z - OFFSETS[o]) & (ZS - 1)) * 4 + (peer & 3)
            o_ref[home] = y[o * chunk : (o + 1) * chunk, :].astype(BF16)


def expert(place, x, own, first, second, rows, parts, back):
    half, wide = own[0].shape
    total = 2 * half
    count = PEERS * ZS * rows
    anyspec = pl.BlockSpec(memory_space=pl.ANY)
    vm = pl.BlockSpec(memory_space=pltpu.VMEM)
    return pl.pallas_call(
        functools.partial(expert_kernel, rows, parts, back),
        in_specs=[pl.BlockSpec(memory_space=pltpu.SMEM)] + [vm] * PEERS + [anyspec] * 9,
        out_specs=vm,
        out_shape=jax.ShapeDtypeStruct((PEERS * ZS, back * rows, wide // back), BF16),
        scratch_shapes=[
            pltpu.VMEM((total, wide), BF16),
            pltpu.VMEM((total, wide), BF16),
            pltpu.VMEM((total, wide), BF16),
            pltpu.VMEM((count, wide), BF16),
            pltpu.VMEM((count // 2, wide), F32),
            pltpu.VMEM((parts * ZS * rows, parts * ZS * rows), BF16),
            pltpu.VMEM((back * ZS * rows, back * ZS * rows), BF16),
            pltpu.SemaphoreType.DMA((9,)),
        ],
        compiler_params=pltpu.CompilerParams(vmem_limit_bytes=60 * 1024 * 1024),
        cost_estimate=pl.CostEstimate(
            flops=6 * count * total * wide,
            bytes_accessed=6 * total * wide + 4 * count * wide,
            transcendentals=count * total,
        ),
        name="expert",
    )(place, *x, *own, *first, *second)


def out_kernel(index_ref, in_ref, out_ref):
    def one(i, _):
        out_ref[i] = in_ref[:, index_ref[i]]
        return 0

    lax.fori_loop(0, out_ref.shape[0], one, 0)


def gather_out(index, cache):
    layers, _, blk, wide = cache.shape
    slots = index.shape[0]
    vm = pl.BlockSpec(memory_space=pltpu.VMEM)
    return pl.pallas_call(
        out_kernel,
        in_specs=[pl.BlockSpec(memory_space=pltpu.SMEM), vm],
        out_specs=vm,
        out_shape=jax.ShapeDtypeStruct((slots, layers, blk, wide), cache.dtype),
        name="gather_out",
    )(index, cache)


def in_kernel(index_ref, in_ref, out_ref):
    def one(i, _):
        out_ref[:, i] = in_ref[index_ref[i]]
        return 0

    lax.fori_loop(0, out_ref.shape[1], one, 0)


def gather_in(index, arrived):
    slots = index.shape[0]
    _, layers, blk, wide = arrived.shape
    vm = pl.BlockSpec(memory_space=pltpu.VMEM)
    return pl.pallas_call(
        in_kernel,
        in_specs=[pl.BlockSpec(memory_space=pltpu.SMEM), vm],
        out_specs=vm,
        out_shape=jax.ShapeDtypeStruct((layers, slots, blk, wide), arrived.dtype),
        name="gather_in",
    )(index, arrived)


def handover_indices(handover_table, sources, blk_dev, spare):
    column = lax.dynamic_index_in_dim(handover_table, lax.axis_index("tp"), 0, keepdims=False)
    here = lax.axis_index("pre")
    table = column.reshape(sources, blk_dev)
    dest = table // blk_dev
    earlier = jnp.arange(blk_dev)[:, None] < jnp.arange(blk_dev)[None, :]
    same = dest[:, :, None] == dest[:, None, :]
    rank = jnp.sum((same & earlier[None]).astype(jnp.int32), axis=1)
    my_dest = lax.dynamic_index_in_dim(dest, here, 0, keepdims=False)
    my_rank = lax.dynamic_index_in_dim(rank, here, 0, keepdims=False)
    wanted = jnp.arange(sources * spare, dtype=jnp.int32)
    out_index = jnp.sum(
        jnp.where(
            wanted[:, None] == (my_dest * spare + my_rank)[None, :],
            jnp.arange(blk_dev, dtype=jnp.int32)[None, :],
            0,
        ),
        axis=1,
    )
    place = here * blk_dev + jnp.arange(blk_dev, dtype=jnp.int32)
    came = jnp.arange(sources, dtype=jnp.int32)[:, None] * spare + rank
    in_index = jnp.sum(
        jnp.where(place[:, None, None] == table[None], came[None], 0), axis=(1, 2)
    )
    return out_index, in_index


def shards(
    tokens,
    route_ids,
    route_weights,
    gate_weight,
    up_weight,
    down_weight,
    prefill_cache,
    handover_table,
):
    tok_dev, wide = tokens.shape
    top_count = route_ids.shape[1]
    tp = lax.axis_size("tp")
    groups = lax.axis_size("pre") * tp
    experts_all = groups // 2
    rows = min(tok_dev, 2 * tok_dev * top_count // experts_all)

    half = down_weight.shape[0]
    quarter = half // 2
    core = lax.axis_index("dec")
    swap = [(i, i ^ 1) for i in range(tp)]
    first, second = [], []
    own = (gate_weight.T, up_weight.T, down_weight)
    for weight in own:
        piece = lax.dynamic_slice_in_dim(weight, core * quarter, quarter, 0)
        got = lax.ppermute(piece, "tp", swap)
        first.append(got)
        second.append(lax.ppermute(got, "dec", [(0, 1), (1, 0)]))

    pre = lax.axis_size("pre")
    lanes = jnp.pad(route_ids.astype(BF16), ((0, 0), (0, 128 - top_count)))
    block = jnp.concatenate([tokens, lanes], axis=1)
    up = [(i, i // ZS * ZS + (i + 1) % ZS) for i in range(pre)]
    down = [(j, i) for i, j in up]
    forward, backward = [block], [block]
    for n in range(4):
        forward.append(lax.ppermute(forward[-1], "pre", up))
        if n < 3:
            backward.append(lax.ppermute(backward[-1], "pre", down))
    blocks = forward + backward[1:]

    here = lax.axis_index("pre")
    there = lax.axis_index("tp")
    me = (here // ZS) * 4 + there // 2
    place = jnp.stack([me, here % ZS]).astype(jnp.int32)
    parts, back = 4, 2
    packed = pack(place, blocks, wide, rows, parts)

    def peer_of(group, flip):
        p, t = group // tp, group % tp
        kind = (t ^ (t >> 1)) & 1
        peer = ((p // ZS) * 4 + t // 2) ^ flip
        high = peer & 1
        return ((peer >> 2) * ZS + p % ZS) * tp + ((peer >> 1) & 1) * 4 + high * 2 + (high ^ kind)

    came = [packed[0]]
    for m in range(1, PEERS):
        came.append(
            lax.ppermute(packed[m], ("pre", "tp"), [(g, peer_of(g, m)) for g in range(groups)])
        )
    came = [c.reshape(-1, wide // parts) for c in came]
    result = expert(place, came, own, first, second, rows, parts, back)

    kinds = [[g for g in range(groups) if (g ^ (g >> 1)) & 1 == kind] for kind in (0, 1)]
    returned = lax.all_to_all(
        result, ("pre", "tp"), split_axis=0, concat_axis=0, axis_index_groups=kinds, tiled=True
    )
    moe_output = combine(
        route_ids.T, route_weights.T, returned.reshape(-1, wide // back), experts_all, rows, back
    )

    _, _, blk_dev, _, _ = prefill_cache.shape
    sources = lax.axis_size("pre")
    spare = blk_dev // sources + 1
    out_index, in_index = handover_indices(handover_table, sources, blk_dev, spare)
    leaving = gather_out(out_index, prefill_cache[:, 0])
    arrived = lax.all_to_all(leaving, "pre", split_axis=0, concat_axis=0, tiled=True)
    decode_cache = gather_in(in_index, arrived)[:, None]
    return (moe_output, decode_cache)


def solution(mesh):
    return jax.shard_map(
        shards,
        mesh=mesh,
        in_specs=(
            P(("pre", "tp", "dec"), None),
            P(("pre", "tp", "dec"), None),
            P(("pre", "tp", "dec"), None),
            P(None, ("pre", "tp")),
            P(None, ("pre", "tp")),
            P(("pre", "tp"), None),
            P(None, "tp", "pre", None, "dec"),
            P(),
        ),
        out_specs=(P(("pre", "tp", "dec"), None), P(None, "tp", "pre", None, "dec")),
        check_vma=False,
    )
```

```python
import functools

import jax
import jax.numpy as jnp
from jax import lax
from jax.experimental import pallas as pl
from jax.experimental.pallas import tpu as pltpu
from jax.sharding import PartitionSpec as P


F32 = jnp.float32
BF16 = jnp.bfloat16
TOP = 6
ZS = 8
PEERS = 8
NEAR = ZS // 2


def iota(shape, dim):
    return lax.broadcasted_iota(jnp.int32, shape, dim)


def divide(x, by):
    return ((x.astype(F32) + 0.5) * (1.0 / by)).astype(jnp.int32)


def dot(a, b, contract):
    return lax.dot_general(a, b, (contract, ((), ())), preferred_element_type=F32)


def expert_of(peer, z):
    return (peer >> 2) * 32 + z * 4 + (peer & 3)


def row_keys(group, rows, lanes):
    index = iota((NEAR * rows, lanes), 0)
    source = divide(index, rows)
    return ((group * NEAR + source) * 16 + index - source * rows).astype(F32)


def pack_kernel(rows, place_ref, *refs):
    blocks = refs[:ZS]
    outs = refs[ZS : ZS + PEERS]
    key_ref, whi_ref, wlo_ref, tok = refs[ZS + PEERS :]
    toks = blocks[0].shape[0]
    wide = tok.shape[1]
    experts = key_ref.shape[0]
    me, z = place_ref[0], place_ref[1]
    before, after = iota((toks, toks), 0), iota((toks, toks), 1)
    same = before == after
    tally = jnp.where(same, 64.0, jnp.where(before < after, 1.0, 0.0)).astype(BF16)
    same = same.astype(BF16)
    eids = iota((toks, experts), 1).astype(F32)
    for o, block in enumerate(blocks):
        lanes = block[:, wide : wide + 128].astype(F32)
        named = jnp.zeros((toks, experts), F32)
        high = jnp.zeros((toks, experts), F32)
        low = jnp.zeros((toks, experts), F32)
        for k in range(TOP):
            hit = lanes[:, k : k + 1] == eids
            named = named + jnp.where(hit, 1.0, 0.0)
            high = high + jnp.where(hit, lanes[:, TOP + k : TOP + k + 1], 0.0)
            low = low + jnp.where(hit, lanes[:, 2 * TOP + k : 2 * TOP + k + 1], 0.0)
        rank = dot(named.astype(BF16), tally, ((0,), (0,))) - 64.0
        here = slice(o * toks, (o + 1) * toks)
        key_ref[:, here] = jnp.where((rank > -0.5) & (rank < rows), rank + 16.0 * o, -1.0)
        whi_ref[:, here] = dot(high.astype(BF16), same, ((0,), (0,)))
        wlo_ref[:, here] = dot(low.astype(BF16), same, ((0,), (0,)))
        tok[here, :] = block[:, :wide]

    span = NEAR * toks
    part = NEAR * rows
    for g in range(ZS // NEAR):
        keys = row_keys(g, rows, span)
        masks = []
        for m in range(PEERS):
            row = key_ref[pl.ds(expert_of(me ^ m, z), 1), g * span : (g + 1) * span]
            masks.append(jnp.where(row == keys, 1.0, 0.0).astype(BF16))
        mask = jnp.concatenate(masks, axis=0)

        def columns(c, _):
            here = pl.ds(pl.multiple_of(c * 512, 512), 512)
            y = dot(mask, tok[g * span : (g + 1) * span, here], ((1,), (0,)))
            for m, out in enumerate(outs):
                out[g * part : (g + 1) * part, here] = y[m * part : (m + 1) * part, :].astype(BF16)
            return 0

        lax.fori_loop(0, wide // 512, columns, 0)


def pack(place, blocks, wide, experts, rows):
    toks = blocks[0].shape[0]
    shape = jax.ShapeDtypeStruct((ZS * rows, wide), BF16)
    small = jax.ShapeDtypeStruct((experts, ZS * toks), F32)
    vm = pl.BlockSpec(memory_space=pltpu.VMEM)
    return pl.pallas_call(
        functools.partial(pack_kernel, rows),
        in_specs=[pl.BlockSpec(memory_space=pltpu.SMEM)] + [vm] * ZS,
        out_specs=[vm] * (PEERS + 3),
        out_shape=[shape] * PEERS + [small] * 3,
        scratch_shapes=[pltpu.VMEM((ZS * toks, wide), BF16)],
        name="pack",
    )(place, *blocks)


def weigh_kernel(rows, group, place_ref, key_ref, whi_ref, wlo_ref, ret_ref, *outs):
    z = place_ref[1]
    span = key_ref.shape[1]
    toks = outs[0].shape[0]
    keys = row_keys(group, rows, span)
    pieces = []
    for j in range(PEERS):
        e = expert_of(j, z)
        hit = key_ref[pl.ds(e, 1), :] == keys
        high = jnp.where(hit, whi_ref[pl.ds(e, 1), :], 0.0).astype(BF16)
        low = jnp.where(hit, wlo_ref[pl.ds(e, 1), :], 0.0).astype(BF16)
        pieces.append(jnp.concatenate([high, low], axis=1))
    left = jnp.concatenate(pieces, axis=0)

    def columns(c, _):
        here = pl.ds(pl.multiple_of(c * 512, 512), 512)
        y = dot(left, ret_ref[:, here], ((0,), (0,)))
        y = y[:span] + y[span:]
        for o, out in enumerate(outs):
            out[:, here] = y[o * toks : (o + 1) * toks, :].astype(out.dtype)
        return 0

    lax.fori_loop(0, ret_ref.shape[1] // 512, columns, 0)


def weigh(place, keys, whi, wlo, ret, group, rows, kinds):
    experts, lanes = keys.shape
    toks = lanes // ZS
    small = pl.BlockSpec((experts, lanes * NEAR // ZS), lambda i: (0, group))
    wide = ret.shape[1]
    return pl.pallas_call(
        functools.partial(weigh_kernel, rows, group),
        grid=(1,),
        in_specs=[
            pl.BlockSpec(memory_space=pltpu.SMEM),
            small,
            small,
            small,
            pl.BlockSpec(ret.shape, lambda i: (0, 0)),
        ],
        out_specs=[pl.BlockSpec((toks, wide), lambda i: (0, 0))] * NEAR,
        out_shape=[jax.ShapeDtypeStruct((toks, wide), kind) for kind in kinds],
        name="weigh",
    )(place, keys, whi, wlo, ret)


def expert_kernel(place_ref, *refs):
    xin = refs[:PEERS]
    g0, u0, d0, g1, u1, d1, g2, u2, d2 = refs[PEERS : PEERS + 9]
    o_ref, wg, wu, wd, xs, acc, sems = refs[PEERS + 9 :]
    half = g0.shape[0]
    quarter = g1.shape[0]
    copies = []
    for i, (src, dst, start) in enumerate(
        [
            (g0, wg, 0),
            (u0, wu, 0),
            (d0, wd, 0),
            (g1, wg, half),
            (u1, wu, half),
            (g2, wg, half + quarter),
            (u2, wu, half + quarter),
            (d1, wd, half),
            (d2, wd, half + quarter),
        ]
    ):
        copy = pltpu.make_async_copy(src, dst.at[pl.ds(start, src.shape[0])], sems.at[i])
        copy.start()
        copies.append(copy)

    part = xin[0].shape[0]
    for m in range(PEERS):
        xs[m * part : (m + 1) * part, :] = xin[m][...]

    me = place_ref[0]
    total = wg.shape[0]
    cuts = [(0, 512), (512, half), (half, half + 512), (half + 512, total)]
    for n, (lo, hi) in enumerate(cuts):
        if n == 0:
            for copy in copies[:3]:
                copy.wait()
        if n == 2:
            for copy in copies[3:]:
                copy.wait()
        x = xs[...]
        gate = dot(x, wg[lo:hi, :], ((1,), (1,)))
        upper = dot(x, wu[lo:hi, :], ((1,), (1,)))
        hidden = (gate / (1.0 + jnp.exp(-gate)) * upper).astype(BF16)
        res = dot(hidden, wd[lo:hi, :], ((1,), (0,)))
        if n == 0:
            acc[...] = res
        elif n < len(cuts) - 1:
            acc[...] = acc[...] + res
        else:
            acc[...] = acc[...] + res
            for m in range(PEERS):
                o_ref[me ^ m] = acc[m * part : (m + 1) * part, :].astype(BF16)


def expert(place, x, own, first, second, group, rows):
    half, wide = own[0].shape
    total = 2 * half
    part = NEAR * rows
    count = PEERS * part
    anyspec = pl.BlockSpec(memory_space=pl.ANY)
    return pl.pallas_call(
        expert_kernel,
        grid=(1,),
        in_specs=[pl.BlockSpec(memory_space=pltpu.SMEM)]
        + [pl.BlockSpec((part, wide), lambda i: (group, 0))] * PEERS
        + [anyspec] * 9,
        out_specs=pl.BlockSpec((PEERS, part, wide), lambda i: (0, 0, 0)),
        out_shape=jax.ShapeDtypeStruct((PEERS, part, wide), BF16),
        scratch_shapes=[
            pltpu.VMEM((total, wide), BF16),
            pltpu.VMEM((total, wide), BF16),
            pltpu.VMEM((total, wide), BF16),
            pltpu.VMEM((count, wide), BF16),
            pltpu.VMEM((count, wide), F32),
            pltpu.SemaphoreType.DMA((9,)),
        ],
        compiler_params=pltpu.CompilerParams(vmem_limit_bytes=60 * 1024 * 1024),
        cost_estimate=pl.CostEstimate(
            flops=6 * count * total * wide,
            bytes_accessed=6 * total * wide + 4 * count * wide,
            transcendentals=count * total,
        ),
        name="expert",
    )(place, *x, *own, *first, *second)


def out_kernel(index_ref, in_ref, out_ref):
    def one(i, _):
        out_ref[i] = in_ref[:, index_ref[i]]
        return 0

    lax.fori_loop(0, out_ref.shape[0], one, 0)


def gather_out(index, cache):
    layers, _, blk, wide = cache.shape
    slots = index.shape[0]
    vm = pl.BlockSpec(memory_space=pltpu.VMEM)
    return pl.pallas_call(
        out_kernel,
        in_specs=[pl.BlockSpec(memory_space=pltpu.SMEM), vm],
        out_specs=vm,
        out_shape=jax.ShapeDtypeStruct((slots, layers, blk, wide), cache.dtype),
        name="gather_out",
    )(index, cache)


def in_kernel(index_ref, in_ref, out_ref):
    def one(i, _):
        out_ref[:, i] = in_ref[index_ref[i]]
        return 0

    lax.fori_loop(0, out_ref.shape[1], one, 0)


def gather_in(index, arrived):
    slots = index.shape[0]
    _, layers, blk, wide = arrived.shape
    vm = pl.BlockSpec(memory_space=pltpu.VMEM)
    return pl.pallas_call(
        in_kernel,
        in_specs=[pl.BlockSpec(memory_space=pltpu.SMEM), vm],
        out_specs=vm,
        out_shape=jax.ShapeDtypeStruct((layers, slots, blk, wide), arrived.dtype),
        name="gather_in",
    )(index, arrived)


def handover_indices(handover_table, sources, blk_dev, spare):
    column = lax.dynamic_index_in_dim(handover_table, lax.axis_index("tp"), 0, keepdims=False)
    here = lax.axis_index("pre")
    table = column.reshape(sources, blk_dev)
    dest = table // blk_dev
    earlier = jnp.arange(blk_dev)[:, None] < jnp.arange(blk_dev)[None, :]
    same = dest[:, :, None] == dest[:, None, :]
    rank = jnp.sum((same & earlier[None]).astype(jnp.int32), axis=1)
    my_dest = lax.dynamic_index_in_dim(dest, here, 0, keepdims=False)
    my_rank = lax.dynamic_index_in_dim(rank, here, 0, keepdims=False)
    wanted = jnp.arange(sources * spare, dtype=jnp.int32)
    out_index = jnp.sum(
        jnp.where(
            wanted[:, None] == (my_dest * spare + my_rank)[None, :],
            jnp.arange(blk_dev, dtype=jnp.int32)[None, :],
            0,
        ),
        axis=1,
    )
    place = here * blk_dev + jnp.arange(blk_dev, dtype=jnp.int32)
    came = jnp.arange(sources, dtype=jnp.int32)[:, None] * spare + rank
    in_index = jnp.sum(
        jnp.where(place[:, None, None] == table[None], came[None], 0), axis=(1, 2)
    )
    return out_index, in_index


def shards(
    tokens,
    route_ids,
    route_weights,
    gate_weight,
    up_weight,
    down_weight,
    prefill_cache,
    handover_table,
):
    tok_dev, wide = tokens.shape
    top_count = route_ids.shape[1]
    tp = lax.axis_size("tp")
    groups = lax.axis_size("pre") * tp
    experts_all = groups // 2
    rows = min(tok_dev, 2 * tok_dev * top_count // experts_all)

    half = down_weight.shape[0]
    quarter = half // 2
    core = lax.axis_index("dec")
    swap = [(i, i ^ 1) for i in range(tp)]
    first, second = [], []
    own = (gate_weight.T, up_weight.T, down_weight)
    for weight in own:
        piece = lax.dynamic_slice_in_dim(weight, core * quarter, quarter, 0)
        got = lax.ppermute(piece, "tp", swap)
        first.append(got)
        second.append(lax.ppermute(got, "dec", [(0, 1), (1, 0)]))

    pre = lax.axis_size("pre")
    high = route_weights.astype(BF16)
    low = (route_weights - high.astype(F32)).astype(BF16)
    lanes = jnp.concatenate([route_ids.astype(BF16), high, low], axis=1)
    lanes = jnp.pad(lanes, ((0, 0), (0, 128 - 3 * top_count)))
    block = jnp.concatenate([tokens, lanes], axis=1)
    up = [(i, i // ZS * ZS + (i + 1) % ZS) for i in range(pre)]
    down = [(j, i) for i, j in up]
    below, above = [block], [block]
    for n in range(4):
        below.append(lax.ppermute(below[-1], "pre", up))
        if n < 3:
            above.append(lax.ppermute(above[-1], "pre", down))
    blocks = [below[4], below[3], above[3], below[2], above[2], below[1], above[1], block]

    here = lax.axis_index("pre")
    there = lax.axis_index("tp")
    me = (here // ZS) * 4 + there // 2
    place = jnp.stack([me, here % ZS]).astype(jnp.int32)
    *packed, keys, whi, wlo = pack(place, blocks, wide, experts_all, rows)

    def kind_of(group):
        return (group ^ (group >> 1)) & 1

    def peer_of(group, flip):
        p, t = group // tp, group % tp
        peer = ((p // ZS) * 4 + t // 2) ^ flip
        last = peer & 1
        return ((peer >> 2) * ZS + p % ZS) * tp + (peer & 2) * 2 + last * 2 + (last ^ kind_of(t))

    came = [packed[0]]
    for m in range(1, PEERS):
        came.append(
            lax.ppermute(packed[m], ("pre", "tp"), [(g, peer_of(g, m)) for g in range(groups)])
        )

    planes = [
        [g for g in range(groups) if g // tp % ZS == z and kind_of(g) == kind]
        for z in range(ZS)
        for kind in (0, 1)
    ]
    sums = []
    results = []
    for group in range(ZS // NEAR):
        results.append(expert(place, came, own, first, second, group, rows))
    for group, result in enumerate(results):
        back = lax.all_to_all(
            result,
            ("pre", "tp"),
            split_axis=0,
            concat_axis=0,
            axis_index_groups=planes,
            tiled=True,
        )
        kinds = (BF16, BF16, F32, F32) if group == 0 else (F32,) * NEAR
        sums += weigh(place, keys, whi, wlo, back.reshape(-1, wide), group, rows, kinds)

    rising, falling = sums[0], sums[1]
    for local in (sums[2], sums[4], sums[6], None):
        rising = lax.ppermute(rising, "pre", up)
        if local is not None:
            rising = (rising.astype(F32) + local).astype(BF16)
    for local in (sums[3], sums[5], None):
        falling = lax.ppermute(falling, "pre", down)
        if local is not None:
            falling = (falling.astype(F32) + local).astype(BF16)
    moe_output = (rising.astype(F32) + falling.astype(F32) + sums[7]).astype(BF16)

    _, _, blk_dev, _, _ = prefill_cache.shape
    sources = lax.axis_size("pre")
    spare = blk_dev // sources + 1
    out_index, in_index = handover_indices(handover_table, sources, blk_dev, spare)
    leaving = gather_out(out_index, prefill_cache[:, 0])
    arrived = lax.all_to_all(leaving, "pre", split_axis=0, concat_axis=0, tiled=True)
    decode_cache = gather_in(in_index, arrived)[:, None]
    return (moe_output, decode_cache)


def solution(mesh):


    return jax.shard_map(
        shards,
        mesh=mesh,
        in_specs=(
            P(("pre", "tp", "dec"), None),
            P(("pre", "tp", "dec"), None),
            P(("pre", "tp", "dec"), None),
            P(None, ("pre", "tp")),
            P(None, ("pre", "tp")),
            P(("pre", "tp"), None),
            P(None, "tp", "pre", None, "dec"),
            P(),
        ),
        out_specs=(P(("pre", "tp", "dec"), None), P(None, "tp", "pre", None, "dec")),
        check_vma=False,
    )
```

```python
import functools

import jax
import jax.numpy as jnp
from jax import lax
from jax.experimental import pallas as pl
from jax.experimental.pallas import tpu as pltpu
from jax.sharding import PartitionSpec as P


F32 = jnp.float32
BF16 = jnp.bfloat16
TOP = 6
ZS = 8
PEERS = 8
NEAR = ZS // 2


def iota(shape, dim):
    return lax.broadcasted_iota(jnp.int32, shape, dim)


def divide(x, by):
    return ((x.astype(F32) + 0.5) * (1.0 / by)).astype(jnp.int32)


def dot(a, b, contract):
    return lax.dot_general(a, b, (contract, ((), ())), preferred_element_type=F32)


def expert_of(peer, z):
    return (peer >> 2) * 32 + z * 4 + (peer & 3)


def row_keys(group, rows, lanes):
    index = iota((NEAR * rows, lanes), 0)
    source = divide(index, rows)
    return ((group * NEAR + source) * 16 + index - source * rows).astype(F32)


def pack_kernel(rows, place_ref, *refs):
    blocks = refs[:ZS]
    outs = refs[ZS : ZS + PEERS]
    key_ref, whi_ref, wlo_ref, tok, side = refs[ZS + PEERS :]
    toks = blocks[0].shape[0]
    wide = tok.shape[1]
    experts = key_ref.shape[0]
    me, z = place_ref[0], place_ref[1]
    before, after = iota((toks, toks), 0), iota((toks, toks), 1)
    same = before == after
    tally = jnp.where(same, 64.0, jnp.where(before < after, 1.0, 0.0)).astype(BF16)
    same = same.astype(BF16)
    eids = iota((toks, experts), 1).astype(F32)
    for o, block in enumerate(blocks):
        side[o] = block[:, wide : wide + 128].astype(F32)
        tok[o * toks : (o + 1) * toks, :] = block[:, :wide]

    def route(pair, _):
        keys, highs, lows = [], [], []
        for n in range(2):
            lanes = side[pair * 2 + n]
            named = jnp.zeros((toks, experts), F32)
            high = jnp.zeros((toks, experts), F32)
            low = jnp.zeros((toks, experts), F32)
            for k in range(TOP):
                hit = lanes[:, k : k + 1] == eids
                named = named + jnp.where(hit, 1.0, 0.0)
                high = high + jnp.where(hit, lanes[:, TOP + k : TOP + k + 1], 0.0)
                low = low + jnp.where(hit, lanes[:, 2 * TOP + k : 2 * TOP + k + 1], 0.0)
            rank = dot(named.astype(BF16), tally, ((0,), (0,))) - 64.0
            first = (16 * (pair * 2 + n)).astype(F32)
            keys.append(jnp.where((rank > -0.5) & (rank < rows), rank + first, -1.0))
            highs.append(dot(high.astype(BF16), same, ((0,), (0,))))
            lows.append(dot(low.astype(BF16), same, ((0,), (0,))))
        here = pl.ds(pl.multiple_of(pair * 2 * toks, 2 * toks), 2 * toks)
        key_ref[:, here] = jnp.concatenate(keys, axis=1)
        whi_ref[:, here] = jnp.concatenate(highs, axis=1)
        wlo_ref[:, here] = jnp.concatenate(lows, axis=1)
        return 0

    lax.fori_loop(0, ZS // 2, route, 0)
    span = NEAR * toks
    part = NEAR * rows

    def one(g, _):
        keys = row_keys(g, rows, span)
        lanes = pl.ds(pl.multiple_of(g * span, span), span)
        masks = []
        for m in range(PEERS):
            row = key_ref[pl.ds(expert_of(me ^ m, z), 1), lanes]
            masks.append(jnp.where(row == keys, 1.0, 0.0).astype(BF16))
        mask = jnp.concatenate(masks, axis=0)
        to = pl.ds(pl.multiple_of(g * part, part), part)

        def columns(c, _):
            here = pl.ds(pl.multiple_of(c * 512, 512), 512)
            y = dot(mask, tok[lanes, here], ((1,), (0,)))
            for m, out in enumerate(outs):
                out[to, here] = y[m * part : (m + 1) * part, :].astype(BF16)
            return 0

        lax.fori_loop(0, wide // 512, columns, 0)
        return 0

    lax.fori_loop(0, ZS // NEAR, one, 0)


def pack(place, blocks, wide, experts, rows):
    toks = blocks[0].shape[0]
    shape = jax.ShapeDtypeStruct((ZS * rows, wide), BF16)
    small = jax.ShapeDtypeStruct((experts, ZS * toks), F32)
    vm = pl.BlockSpec(memory_space=pltpu.VMEM)
    return pl.pallas_call(
        functools.partial(pack_kernel, rows),
        in_specs=[pl.BlockSpec(memory_space=pltpu.SMEM)] + [vm] * ZS,
        out_specs=[vm] * (PEERS + 3),
        out_shape=[shape] * PEERS + [small] * 3,
        scratch_shapes=[pltpu.VMEM((ZS * toks, wide), BF16), pltpu.VMEM((ZS, toks, 128), F32)],
        name="pack",
    )(place, *blocks)


def weigh_kernel(rows, group, place_ref, key_ref, whi_ref, wlo_ref, ret_ref, *outs):
    z = place_ref[1]
    span = key_ref.shape[1]
    toks = outs[0].shape[0]
    keys = row_keys(group, rows, span)
    pieces = []
    for j in range(PEERS):
        e = expert_of(j, z)
        hit = key_ref[pl.ds(e, 1), :] == keys
        high = jnp.where(hit, whi_ref[pl.ds(e, 1), :], 0.0).astype(BF16)
        low = jnp.where(hit, wlo_ref[pl.ds(e, 1), :], 0.0).astype(BF16)
        pieces.append(jnp.concatenate([high, low], axis=1))
    left = jnp.concatenate(pieces, axis=0)

    def columns(c, _):
        here = pl.ds(pl.multiple_of(c * 512, 512), 512)
        y = dot(left, ret_ref[:, here], ((0,), (0,)))
        y = y[:span] + y[span:]
        for o, out in enumerate(outs):
            out[:, here] = y[o * toks : (o + 1) * toks, :].astype(out.dtype)
        return 0

    lax.fori_loop(0, ret_ref.shape[1] // 512, columns, 0)


def weigh(place, keys, whi, wlo, ret, group, rows, kinds):
    experts, lanes = keys.shape
    toks = lanes // ZS
    small = pl.BlockSpec((experts, lanes * NEAR // ZS), lambda i: (0, group))
    wide = ret.shape[1]
    return pl.pallas_call(
        functools.partial(weigh_kernel, rows, group),
        grid=(1,),
        in_specs=[
            pl.BlockSpec(memory_space=pltpu.SMEM),
            small,
            small,
            small,
            pl.BlockSpec(ret.shape, lambda i: (0, 0)),
        ],
        out_specs=[pl.BlockSpec((toks, wide), lambda i: (0, 0))] * NEAR,
        out_shape=[jax.ShapeDtypeStruct((toks, wide), kind) for kind in kinds],
        name="weigh",
    )(place, keys, whi, wlo, ret)


def expert_kernel(place_ref, *refs):
    xin = refs[:PEERS]
    g0, u0, d0, g1, u1, d1, g2, u2, d2 = refs[PEERS : PEERS + 9]
    o_ref, wg, wu, wd, xs, acc, sems = refs[PEERS + 9 :]
    half = g0.shape[0]
    quarter = g1.shape[0]
    copies = []
    for i, (src, dst, start) in enumerate(
        [
            (g0, wg, 0),
            (u0, wu, 0),
            (d0, wd, 0),
            (g1, wg, half),
            (u1, wu, half),
            (g2, wg, half + quarter),
            (u2, wu, half + quarter),
            (d1, wd, half),
            (d2, wd, half + quarter),
        ]
    ):
        copy = pltpu.make_async_copy(src, dst.at[pl.ds(start, src.shape[0])], sems.at[i])
        copy.start()
        copies.append(copy)

    part = xin[0].shape[0]
    for m in range(PEERS):
        xs[m * part : (m + 1) * part, :] = xin[m][...]

    me = place_ref[0]
    acc[...] = jnp.zeros_like(acc)
    for copy in copies[:3]:
        copy.wait()

    def run(n, _):
        @pl.when(n == 1)
        def _():
            for copy in copies[3:]:
                copy.wait()

        here = pl.ds(pl.multiple_of(n * half, half), half)
        x = xs[...]
        gate = dot(x, wg[here, :], ((1,), (1,)))
        upper = dot(x, wu[here, :], ((1,), (1,)))
        hidden = (gate / (1.0 + jnp.exp(-gate)) * upper).astype(BF16)
        acc[...] = acc[...] + dot(hidden, wd[here, :], ((1,), (0,)))
        return 0

    lax.fori_loop(0, 2, run, 0)
    for m in range(PEERS):
        o_ref[me ^ m] = acc[m * part : (m + 1) * part, :].astype(BF16)


def expert(place, x, own, first, second, group, rows):
    half, wide = own[0].shape
    total = 2 * half
    part = NEAR * rows
    count = PEERS * part
    anyspec = pl.BlockSpec(memory_space=pl.ANY)
    return pl.pallas_call(
        expert_kernel,
        grid=(1,),
        in_specs=[pl.BlockSpec(memory_space=pltpu.SMEM)]
        + [pl.BlockSpec((part, wide), lambda i: (group, 0))] * PEERS
        + [anyspec] * 9,
        out_specs=pl.BlockSpec((PEERS, part, wide), lambda i: (0, 0, 0)),
        out_shape=jax.ShapeDtypeStruct((PEERS, part, wide), BF16),
        scratch_shapes=[
            pltpu.VMEM((total, wide), BF16),
            pltpu.VMEM((total, wide), BF16),
            pltpu.VMEM((total, wide), BF16),
            pltpu.VMEM((count, wide), BF16),
            pltpu.VMEM((count, wide), F32),
            pltpu.SemaphoreType.DMA((9,)),
        ],
        compiler_params=pltpu.CompilerParams(vmem_limit_bytes=60 * 1024 * 1024),
        cost_estimate=pl.CostEstimate(
            flops=6 * count * total * wide,
            bytes_accessed=6 * total * wide + 4 * count * wide,
            transcendentals=count * total,
        ),
        name="expert",
    )(place, *x, *own, *first, *second)


def leave_kernel(place_ref, table_ref, in_ref, same_ref, cross_ref, used):
    z, x, column = place_ref[1], place_ref[2], place_ref[3]
    blk_dev = in_ref.shape[1]

    def clear(p, _):
        used[p] = 0
        return 0

    lax.fori_loop(0, 2 * ZS, clear, 0)

    def one(i, _):
        dest = table_ref[column, (x * ZS + z) * blk_dev + i] // blk_dev
        rank = used[dest]
        used[dest] = rank + 1
        far = dest & (ZS - 1)

        @pl.when(dest // ZS == x)
        def _():
            same_ref[far, rank] = in_ref[:, i]

        @pl.when(dest // ZS != x)
        def _():
            cross_ref[(far - z) & (ZS - 1), rank] = in_ref[:, i]

        return 0

    lax.fori_loop(0, blk_dev, one, 0)


def gather_out(place, table, cache, spare):
    layers, _, blk, wide = cache.shape
    smem = pl.BlockSpec(memory_space=pltpu.SMEM)
    vm = pl.BlockSpec(memory_space=pltpu.VMEM)
    shape = jax.ShapeDtypeStruct((ZS, spare, layers, blk, wide), cache.dtype)
    return pl.pallas_call(
        leave_kernel,
        in_specs=[smem, smem, vm],
        out_specs=[vm, vm],
        out_shape=[shape, shape],
        scratch_shapes=[pltpu.SMEM((2 * ZS,), jnp.int32)],
        name="gather_out",
    )(place, table, cache)


def arrive_kernel(place_ref, slot_ref, same_ref, *refs):
    crossed, out_ref = refs[:ZS], refs[ZS]
    z, x = place_ref[1], place_ref[2]
    spare = same_ref.shape[1]

    def put(source, i, ref):
        to = slot_ref[source * spare + i]

        @pl.when(to >= 0)
        def _():
            out_ref[:, to] = ref[...]

    def one(n, _):
        for i in range(spare):
            put(x * ZS + n, i, same_ref.at[n, i])
        return 0

    lax.fori_loop(0, ZS, one, 0)
    for n in range(ZS):
        for i in range(spare):
            put((1 - x) * ZS + ((z - n) & (ZS - 1)), i, crossed[n].at[i])


def gather_in(place, slots, same, crossed, blk_dev):
    _, _, layers, blk, wide = same.shape
    smem = pl.BlockSpec(memory_space=pltpu.SMEM)
    vm = pl.BlockSpec(memory_space=pltpu.VMEM)
    return pl.pallas_call(
        arrive_kernel,
        in_specs=[smem, smem] + [vm] * (ZS + 1),
        out_specs=vm,
        out_shape=jax.ShapeDtypeStruct((layers, blk_dev, blk, wide), same.dtype),
        name="gather_in",
    )(place, slots, same, *crossed)


def arrival_slots(handover_table, sources, blk_dev, spare):
    column = lax.dynamic_index_in_dim(handover_table, lax.axis_index("tp"), 0, keepdims=False)
    here = lax.axis_index("pre")
    table = column.reshape(sources, blk_dev)
    dest = table // blk_dev
    earlier = jnp.arange(blk_dev)[:, None] < jnp.arange(blk_dev)[None, :]
    same = dest[:, :, None] == dest[:, None, :]
    rank = jnp.sum((same & earlier[None]).astype(jnp.int32), axis=1)
    wanted = jnp.arange(sources * spare, dtype=jnp.int32)
    came = jnp.arange(sources, dtype=jnp.int32)[:, None] * spare + rank
    came = jnp.where(dest == here, came, -1).reshape(-1)
    slots = jnp.where(wanted[:, None] == came[None, :], (column % blk_dev + 1)[None, :], 0)
    return jnp.sum(slots, axis=1) - 1


def shards(
    tokens,
    route_ids,
    route_weights,
    gate_weight,
    up_weight,
    down_weight,
    prefill_cache,
    handover_table,
):
    tok_dev, wide = tokens.shape
    top_count = route_ids.shape[1]
    tp = lax.axis_size("tp")
    groups = lax.axis_size("pre") * tp
    experts_all = groups // 2
    rows = min(tok_dev, 2 * tok_dev * top_count // experts_all)

    half = down_weight.shape[0]
    quarter = half // 2
    core = lax.axis_index("dec")
    swap = [(i, i ^ 1) for i in range(tp)]
    first, second = [], []
    own = (gate_weight.T, up_weight.T, down_weight)
    for weight in own:
        piece = lax.dynamic_slice_in_dim(weight, core * quarter, quarter, 0)
        got = lax.ppermute(piece, "tp", swap)
        first.append(got)
        second.append(lax.ppermute(got, "dec", [(0, 1), (1, 0)]))

    pre = lax.axis_size("pre")
    high = route_weights.astype(BF16)
    low = (route_weights - high.astype(F32)).astype(BF16)
    lanes = jnp.concatenate([route_ids.astype(BF16), high, low], axis=1)
    lanes = jnp.pad(lanes, ((0, 0), (0, 128 - 3 * top_count)))
    block = jnp.concatenate([tokens, lanes], axis=1)
    up = [(i, i // ZS * ZS + (i + 1) % ZS) for i in range(pre)]
    down = [(j, i) for i, j in up]
    below, above = [block], [block]
    for n in range(4):
        below.append(lax.ppermute(below[-1], "pre", up))
        if n < 3:
            above.append(lax.ppermute(above[-1], "pre", down))
    blocks = [below[4], below[3], above[3], below[2], above[2], below[1], above[1], block]

    here = lax.axis_index("pre")
    there = lax.axis_index("tp")
    me = (here // ZS) * 4 + there // 2
    place = jnp.stack([me, here % ZS, here // ZS, there]).astype(jnp.int32)
    *packed, keys, whi, wlo = pack(place, blocks, wide, experts_all, rows)

    def kind_of(group):
        return (group ^ (group >> 1)) & 1

    def peer_of(group, flip):
        p, t = group // tp, group % tp
        peer = ((p // ZS) * 4 + t // 2) ^ flip
        last = peer & 1
        return ((peer >> 2) * ZS + p % ZS) * tp + (peer & 2) * 2 + last * 2 + (last ^ kind_of(t))

    came = [packed[0]]
    for m in range(1, PEERS):
        came.append(
            lax.ppermute(packed[m], ("pre", "tp"), [(g, peer_of(g, m)) for g in range(groups)])
        )

    planes = [
        [g for g in range(groups) if g // tp % ZS == z and kind_of(g) == kind]
        for z in range(ZS)
        for kind in (0, 1)
    ]
    sums = []
    results = []
    for group in range(ZS // NEAR):
        results.append(expert(place, came, own, first, second, group, rows))
    for group, result in enumerate(results):
        back = lax.all_to_all(
            result,
            ("pre", "tp"),
            split_axis=0,
            concat_axis=0,
            axis_index_groups=planes,
            tiled=True,
        )
        kinds = (BF16, BF16, F32, F32) if group == 0 else (F32,) * NEAR
        sums += weigh(place, keys, whi, wlo, back.reshape(-1, wide), group, rows, kinds)

    rising, falling = sums[0], sums[1]
    for local in (sums[2], sums[4], sums[6], None):
        rising = lax.ppermute(rising, "pre", up)
        if local is not None:
            rising = (rising.astype(F32) + local).astype(BF16)
    for local in (sums[3], sums[5], None):
        falling = lax.ppermute(falling, "pre", down)
        if local is not None:
            falling = (falling.astype(F32) + local).astype(BF16)
    moe_output = (rising.astype(F32) + falling.astype(F32) + sums[7]).astype(BF16)

    _, _, blk_dev, _, _ = prefill_cache.shape
    sources = lax.axis_size("pre")
    spare = blk_dev // sources + 1
    in_slots = arrival_slots(handover_table, sources, blk_dev, spare)
    same, cross = gather_out(place, handover_table, prefill_cache[:, 0], spare)
    cross = lax.ppermute(cross, "pre", [(i, (i + ZS) % sources) for i in range(sources)])
    same = lax.all_to_all(
        same,
        "pre",
        split_axis=0,
        concat_axis=0,
        axis_index_groups=[list(range(x * ZS, (x + 1) * ZS)) for x in range(sources // ZS)],
        tiled=True,
    )
    crossed = [cross[0]]
    for n in range(1, ZS):
        crossed.append(
            lax.ppermute(
                cross[n], "pre", [(i, i // ZS * ZS + (i + n) % ZS) for i in range(sources)]
            )
        )
    decode_cache = gather_in(place, in_slots, same, crossed, blk_dev)[:, None]
    return (moe_output, decode_cache)


def solution(mesh):


    return jax.shard_map(
        shards,
        mesh=mesh,
        in_specs=(
            P(("pre", "tp", "dec"), None),
            P(("pre", "tp", "dec"), None),
            P(("pre", "tp", "dec"), None),
            P(None, ("pre", "tp")),
            P(None, ("pre", "tp")),
            P(("pre", "tp"), None),
            P(None, "tp", "pre", None, "dec"),
            P(),
        ),
        out_specs=(P(("pre", "tp", "dec"), None), P(None, "tp", "pre", None, "dec")),
        check_vma=False,
    )
```

```python
import functools

import jax
import jax.numpy as jnp
from jax import lax
from jax.experimental import pallas as pl
from jax.experimental.pallas import tpu as pltpu
from jax.sharding import PartitionSpec as P


F32 = jnp.float32
BF16 = jnp.bfloat16
TOP = 6
ZS = 8
PEERS = 8
NEAR = ZS // 2


def iota(shape, dim):
    return lax.broadcasted_iota(jnp.int32, shape, dim)


def divide(x, by):
    return ((x.astype(F32) + 0.5) * (1.0 / by)).astype(jnp.int32)


def dot(a, b, contract):
    return lax.dot_general(a, b, (contract, ((), ())), preferred_element_type=F32)


def expert_of(peer, z):
    return (peer >> 2) * 32 + z * 4 + (peer & 3)


def row_keys(rows, lanes):
    index = iota((NEAR * rows, lanes), 0)
    source = divide(index, rows)
    return (source * 16 + index - source * rows).astype(F32)


def pack_kernel(rows, ready, place_ref, *refs):
    blocks = refs[:NEAR]
    early = refs[NEAR : NEAR + ready]
    outs = refs[NEAR + ready : NEAR + ready + PEERS]
    key_ref, whi_ref, wlo_ref, tok, side, mask = refs[NEAR + ready + PEERS :]
    toks = blocks[0].shape[0]
    wide = tok.shape[1]
    experts = key_ref.shape[0]
    me, z = place_ref[0], place_ref[1]
    before, after = iota((toks, toks), 0), iota((toks, toks), 1)
    same = before == after
    tally = jnp.where(same, 64.0, jnp.where(before < after, 1.0, 0.0)).astype(BF16)
    same = same.astype(BF16)
    eids = iota((toks, experts), 1).astype(F32)
    for o, block in enumerate(blocks):
        side[o] = block[:, wide : wide + 128].astype(F32)
        tok[o * toks : (o + 1) * toks, :] = block[:, :wide]

    def route(pair, _):
        keys, highs, lows = [], [], []
        for n in range(2):
            lanes = side[pair * 2 + n]
            named = jnp.zeros((toks, experts), F32)
            high = jnp.zeros((toks, experts), F32)
            low = jnp.zeros((toks, experts), F32)
            for k in range(TOP):
                hit = lanes[:, k : k + 1] == eids
                named = named + jnp.where(hit, 1.0, 0.0)
                high = high + jnp.where(hit, lanes[:, TOP + k : TOP + k + 1], 0.0)
                low = low + jnp.where(hit, lanes[:, 2 * TOP + k : 2 * TOP + k + 1], 0.0)
            rank = dot(named.astype(BF16), tally, ((0,), (0,))) - 64.0
            first = (16 * (pair * 2 + n)).astype(F32)
            keys.append(jnp.where((rank > -0.5) & (rank < rows), rank + first, -1.0))
            highs.append(dot(high.astype(BF16), same, ((0,), (0,))))
            lows.append(dot(low.astype(BF16), same, ((0,), (0,))))
        here = pl.ds(pl.multiple_of(pair * 2 * toks, 2 * toks), 2 * toks)
        key_ref[:, here] = jnp.concatenate(keys, axis=1)
        whi_ref[:, here] = jnp.concatenate(highs, axis=1)
        wlo_ref[:, here] = jnp.concatenate(lows, axis=1)
        return 0

    lax.fori_loop(0, NEAR // 2, route, 0)
    part = NEAR * rows
    keys = row_keys(rows, NEAR * toks)

    def fill(m, _):
        row = key_ref[pl.ds(expert_of(me ^ m, z), 1), :]
        to = pl.ds(pl.multiple_of(m * part, part), part)
        mask[to, :] = jnp.where(row == keys, 1.0, 0.0).astype(BF16)
        return 0

    lax.fori_loop(0, PEERS, fill, 0)

    def columns(c, _):
        here = pl.ds(pl.multiple_of(c * 512, 512), 512)
        y = dot(mask[...], tok[:, here], ((1,), (0,)))
        for m, out in enumerate(outs):
            out[:part, here] = y[m * part : (m + 1) * part, :].astype(BF16)
        return 0

    lax.fori_loop(0, wide // 512, columns, 0)
    for out, ref in zip(outs, early):
        out[part:, :] = ref[...]


def pack(place, blocks, early, wide, experts, rows):
    toks = blocks[0].shape[0]
    groups = 2 if early else 1
    shape = jax.ShapeDtypeStruct((groups * NEAR * rows, wide), BF16)
    small = jax.ShapeDtypeStruct((experts, NEAR * toks), F32)
    vm = pl.BlockSpec(memory_space=pltpu.VMEM)
    return pl.pallas_call(
        functools.partial(pack_kernel, rows, len(early)),
        in_specs=[pl.BlockSpec(memory_space=pltpu.SMEM)] + [vm] * (NEAR + len(early)),
        out_specs=[vm] * (PEERS + 3),
        out_shape=[shape] * PEERS + [small] * 3,
        scratch_shapes=[
            pltpu.VMEM((NEAR * toks, wide), BF16),
            pltpu.VMEM((NEAR, toks, 128), F32),
            pltpu.VMEM((PEERS * NEAR * rows, NEAR * toks), BF16),
        ],
        name="pack",
    )(place, *blocks, *early)


def weigh_kernel(rows, place_ref, key_ref, whi_ref, wlo_ref, ret_ref, *refs):
    *outs, left = refs
    z = place_ref[1]
    span = key_ref.shape[1]
    toks = outs[0].shape[0]
    keys = row_keys(rows, span)
    part = keys.shape[0]

    def fill(j, _):
        e = expert_of(j, z)
        to = pl.ds(pl.multiple_of(j * part, part), part)
        hit = key_ref[pl.ds(e, 1), :] == keys
        left[to, :span] = jnp.where(hit, whi_ref[pl.ds(e, 1), :], 0.0).astype(BF16)
        left[to, span:] = jnp.where(hit, wlo_ref[pl.ds(e, 1), :], 0.0).astype(BF16)
        return 0

    lax.fori_loop(0, PEERS, fill, 0)

    def columns(c, _):
        here = pl.ds(pl.multiple_of(c * 512, 512), 512)
        y = dot(left[...], ret_ref[:, here], ((0,), (0,)))
        y = y[:span] + y[span:]
        for o, out in enumerate(outs):
            out[:, here] = y[o * toks : (o + 1) * toks, :].astype(out.dtype)
        return 0

    lax.fori_loop(0, ret_ref.shape[1] // 512, columns, 0)


def weigh(place, keys, whi, wlo, ret, rows, kinds):
    _, lanes = keys.shape
    toks = lanes // NEAR
    wide = ret.shape[1]
    vm = pl.BlockSpec(memory_space=pltpu.VMEM)
    return pl.pallas_call(
        functools.partial(weigh_kernel, rows),
        in_specs=[pl.BlockSpec(memory_space=pltpu.SMEM)] + [vm] * 4,
        out_specs=[vm] * NEAR,
        out_shape=[jax.ShapeDtypeStruct((toks, wide), kind) for kind in kinds],
        scratch_shapes=[pltpu.VMEM((ret.shape[0], 2 * lanes), BF16)],
        name="weigh",
    )(place, keys, whi, wlo, ret)


def expert_kernel(place_ref, *refs):
    xin = refs[:PEERS]
    g0, u0, d0, g1, u1, d1, g2, u2, d2 = refs[PEERS : PEERS + 9]
    o_ref, wg, wu, wd, xs, acc, sems = refs[PEERS + 9 :]
    half = g0.shape[0]
    quarter = g1.shape[0]
    copies = []
    for i, (src, dst, start) in enumerate(
        [
            (g0, wg, 0),
            (u0, wu, 0),
            (d0, wd, 0),
            (g1, wg, half),
            (u1, wu, half),
            (g2, wg, half + quarter),
            (u2, wu, half + quarter),
            (d1, wd, half),
            (d2, wd, half + quarter),
        ]
    ):
        copy = pltpu.make_async_copy(src, dst.at[pl.ds(start, src.shape[0])], sems.at[i])
        copy.start()
        copies.append(copy)

    part = xin[0].shape[0]
    for m in range(PEERS):
        xs[m * part : (m + 1) * part, :] = xin[m][...]

    me = place_ref[0]
    acc[...] = jnp.zeros_like(acc)
    for copy in copies[:3]:
        copy.wait()

    def run(n, _):
        @pl.when(n == 1)
        def _():
            for copy in copies[3:]:
                copy.wait()

        here = pl.ds(pl.multiple_of(n * half, half), half)
        x = xs[...]
        gate = dot(x, wg[here, :], ((1,), (1,)))
        upper = dot(x, wu[here, :], ((1,), (1,)))
        hidden = (gate / (1.0 + jnp.exp(-gate)) * upper).astype(BF16)
        acc[...] = acc[...] + dot(hidden, wd[here, :], ((1,), (0,)))
        return 0

    lax.fori_loop(0, 2, run, 0)
    for m in range(PEERS):
        o_ref[me ^ m] = acc[m * part : (m + 1) * part, :].astype(BF16)


def expert(place, x, own, first, second, group, rows):
    half, wide = own[0].shape
    total = 2 * half
    part = NEAR * rows
    count = PEERS * part
    anyspec = pl.BlockSpec(memory_space=pl.ANY)
    return pl.pallas_call(
        expert_kernel,
        grid=(1,),
        in_specs=[pl.BlockSpec(memory_space=pltpu.SMEM)]
        + [pl.BlockSpec((part, wide), lambda i: (group, 0))] * PEERS
        + [anyspec] * 9,
        out_specs=pl.BlockSpec((PEERS, part, wide), lambda i: (0, 0, 0)),
        out_shape=jax.ShapeDtypeStruct((PEERS, part, wide), BF16),
        scratch_shapes=[
            pltpu.VMEM((total, wide), BF16),
            pltpu.VMEM((total, wide), BF16),
            pltpu.VMEM((total, wide), BF16),
            pltpu.VMEM((count, wide), BF16),
            pltpu.VMEM((count, wide), F32),
            pltpu.SemaphoreType.DMA((9,)),
        ],
        compiler_params=pltpu.CompilerParams(vmem_limit_bytes=60 * 1024 * 1024),
        cost_estimate=pl.CostEstimate(
            flops=6 * count * total * wide,
            bytes_accessed=6 * total * wide + 4 * count * wide,
            transcendentals=count * total,
        ),
        name="expert",
    )(place, *x, *own, *first, *second)


def leave_kernel(place_ref, table_ref, in_ref, same_ref, cross_ref, used):
    z, x, column = place_ref[1], place_ref[2], place_ref[3]
    blk_dev = in_ref.shape[1]

    def clear(p, _):
        used[p] = 0
        return 0

    lax.fori_loop(0, 2 * ZS, clear, 0)

    def one(i, _):
        dest = table_ref[column, (x * ZS + z) * blk_dev + i] // blk_dev
        rank = used[dest]
        used[dest] = rank + 1
        far = dest & (ZS - 1)

        @pl.when(dest // ZS == x)
        def _():
            same_ref[far, rank] = in_ref[:, i]

        @pl.when(dest // ZS != x)
        def _():
            cross_ref[(far - z) & (ZS - 1), rank] = in_ref[:, i]

        return 0

    lax.fori_loop(0, blk_dev, one, 0)


def gather_out(place, table, cache, spare):
    layers, _, blk, wide = cache.shape
    smem = pl.BlockSpec(memory_space=pltpu.SMEM)
    vm = pl.BlockSpec(memory_space=pltpu.VMEM)
    shape = jax.ShapeDtypeStruct((ZS, spare, layers, blk, wide), cache.dtype)
    return pl.pallas_call(
        leave_kernel,
        in_specs=[smem, smem, vm],
        out_specs=[vm, vm],
        out_shape=[shape, shape],
        scratch_shapes=[pltpu.SMEM((2 * ZS,), jnp.int32)],
        name="gather_out",
    )(place, table, cache)


def arrive_kernel(place_ref, slot_ref, same_ref, *refs):
    crossed, out_ref = refs[:ZS], refs[ZS]
    z, x = place_ref[1], place_ref[2]
    spare = same_ref.shape[1]

    def put(source, i, ref):
        to = slot_ref[source * spare + i]

        @pl.when(to >= 0)
        def _():
            out_ref[:, to] = ref[...]

    def one(n, _):
        for i in range(spare):
            put(x * ZS + n, i, same_ref.at[n, i])
        return 0

    lax.fori_loop(0, ZS, one, 0)
    for n in range(ZS):
        for i in range(spare):
            put((1 - x) * ZS + ((z - n) & (ZS - 1)), i, crossed[n].at[i])


def gather_in(place, slots, same, crossed, blk_dev):
    _, _, layers, blk, wide = same.shape
    smem = pl.BlockSpec(memory_space=pltpu.SMEM)
    vm = pl.BlockSpec(memory_space=pltpu.VMEM)
    return pl.pallas_call(
        arrive_kernel,
        in_specs=[smem, smem] + [vm] * (ZS + 1),
        out_specs=vm,
        out_shape=jax.ShapeDtypeStruct((layers, blk_dev, blk, wide), same.dtype),
        name="gather_in",
    )(place, slots, same, *crossed)


def arrival_slots(handover_table, sources, blk_dev, spare):
    column = lax.dynamic_index_in_dim(handover_table, lax.axis_index("tp"), 0, keepdims=False)
    here = lax.axis_index("pre")
    table = column.reshape(sources, blk_dev)
    dest = table // blk_dev
    earlier = jnp.arange(blk_dev)[:, None] < jnp.arange(blk_dev)[None, :]
    same = dest[:, :, None] == dest[:, None, :]
    rank = jnp.sum((same & earlier[None]).astype(jnp.int32), axis=1)
    wanted = jnp.arange(sources * spare, dtype=jnp.int32)
    came = jnp.arange(sources, dtype=jnp.int32)[:, None] * spare + rank
    came = jnp.where(dest == here, came, -1).reshape(-1)
    slots = jnp.where(wanted[:, None] == came[None, :], (column % blk_dev + 1)[None, :], 0)
    return jnp.sum(slots, axis=1) - 1


def shards(
    tokens,
    route_ids,
    route_weights,
    gate_weight,
    up_weight,
    down_weight,
    prefill_cache,
    handover_table,
):
    tok_dev, wide = tokens.shape
    top_count = route_ids.shape[1]
    tp = lax.axis_size("tp")
    groups = lax.axis_size("pre") * tp
    experts_all = groups // 2
    rows = min(tok_dev, 2 * tok_dev * top_count // experts_all)

    half = down_weight.shape[0]
    quarter = half // 2
    core = lax.axis_index("dec")
    swap = [(i, i ^ 1) for i in range(tp)]
    first, second = [], []
    own = (gate_weight.T, up_weight.T, down_weight)
    for weight in own:
        piece = lax.dynamic_slice_in_dim(weight, core * quarter, quarter, 0)
        got = lax.ppermute(piece, "tp", swap)
        first.append(got)
        second.append(lax.ppermute(got, "dec", [(0, 1), (1, 0)]))

    pre = lax.axis_size("pre")
    high = route_weights.astype(BF16)
    low = (route_weights - high.astype(F32)).astype(BF16)
    lanes = jnp.concatenate([route_ids.astype(BF16), high, low], axis=1)
    lanes = jnp.pad(lanes, ((0, 0), (0, 128 - 3 * top_count)))
    block = jnp.concatenate([tokens, lanes], axis=1)
    up = [(i, i // ZS * ZS + (i + 1) % ZS) for i in range(pre)]
    down = [(j, i) for i, j in up]
    below, above = [block], [block]
    for n in range(4):
        below.append(lax.ppermute(below[-1], "pre", up))
        if n < 3:
            above.append(lax.ppermute(above[-1], "pre", down))
    blocks = [below[4], below[3], above[3], below[2], above[2], below[1], above[1], block]

    here = lax.axis_index("pre")
    there = lax.axis_index("tp")
    me = (here // ZS) * 4 + there // 2
    place = jnp.stack([me, here % ZS, here // ZS, there]).astype(jnp.int32)
    *packed, keys, whi, wlo = pack(place, blocks[NEAR:], [], wide, experts_all, rows)
    routes = [(keys, whi, wlo)]
    *packed, keys, whi, wlo = pack(place, blocks[:NEAR], packed, wide, experts_all, rows)
    routes.insert(0, (keys, whi, wlo))

    def kind_of(group):
        return (group ^ (group >> 1)) & 1

    def peer_of(group, flip):
        p, t = group // tp, group % tp
        peer = ((p // ZS) * 4 + t // 2) ^ flip
        last = peer & 1
        return ((peer >> 2) * ZS + p % ZS) * tp + (peer & 2) * 2 + last * 2 + (last ^ kind_of(t))

    came = [packed[0]]
    for m in range(1, PEERS):
        came.append(
            lax.ppermute(packed[m], ("pre", "tp"), [(g, peer_of(g, m)) for g in range(groups)])
        )

    planes = [
        [g for g in range(groups) if g // tp % ZS == z and kind_of(g) == kind]
        for z in range(ZS)
        for kind in (0, 1)
    ]
    sums = []
    results = []
    for group in range(ZS // NEAR):
        results.append(expert(place, came, own, first, second, group, rows))
    for group, result in enumerate(results):
        back = lax.all_to_all(
            result,
            ("pre", "tp"),
            split_axis=0,
            concat_axis=0,
            axis_index_groups=planes,
            tiled=True,
        )
        kinds = (BF16, BF16, F32, F32) if group == 0 else (F32,) * NEAR
        sums += weigh(place, *routes[group], back.reshape(-1, wide), rows, kinds)

    rising, falling = sums[0], sums[1]
    for local in (sums[2], sums[4], sums[6], None):
        rising = lax.ppermute(rising, "pre", up)
        if local is not None:
            rising = (rising.astype(F32) + local).astype(BF16)
    for local in (sums[3], sums[5], None):
        falling = lax.ppermute(falling, "pre", down)
        if local is not None:
            falling = (falling.astype(F32) + local).astype(BF16)
    moe_output = (rising.astype(F32) + falling.astype(F32) + sums[7]).astype(BF16)

    _, _, blk_dev, _, _ = prefill_cache.shape
    sources = lax.axis_size("pre")
    spare = blk_dev // sources + 1
    in_slots = arrival_slots(handover_table, sources, blk_dev, spare)
    same, cross = gather_out(place, handover_table, prefill_cache[:, 0], spare)
    cross = lax.ppermute(cross, "pre", [(i, (i + ZS) % sources) for i in range(sources)])
    same = lax.all_to_all(
        same,
        "pre",
        split_axis=0,
        concat_axis=0,
        axis_index_groups=[list(range(x * ZS, (x + 1) * ZS)) for x in range(sources // ZS)],
        tiled=True,
    )
    crossed = [cross[0]]
    for n in range(1, ZS):
        crossed.append(
            lax.ppermute(
                cross[n], "pre", [(i, i // ZS * ZS + (i + n) % ZS) for i in range(sources)]
            )
        )
    decode_cache = gather_in(place, in_slots, same, crossed, blk_dev)[:, None]
    return (moe_output, decode_cache)


def solution(mesh):
    return jax.shard_map(
        shards,
        mesh=mesh,
        in_specs=(
            P(("pre", "tp", "dec"), None),
            P(("pre", "tp", "dec"), None),
            P(("pre", "tp", "dec"), None),
            P(None, ("pre", "tp")),
            P(None, ("pre", "tp")),
            P(("pre", "tp"), None),
            P(None, "tp", "pre", None, "dec"),
            P(),
        ),
        out_specs=(P(("pre", "tp", "dec"), None), P(None, "tp", "pre", None, "dec")),
        check_vma=False,
    )
```

```python
import functools

import jax
import jax.numpy as jnp
from jax import lax
from jax.experimental import pallas as pl
from jax.experimental.pallas import tpu as pltpu
from jax.sharding import PartitionSpec as P


F32 = jnp.float32
BF16 = jnp.bfloat16
TOP = 6
ZS = 8
PEERS = 8
NEAR = ZS // 2


def iota(shape, dim):
    return lax.broadcasted_iota(jnp.int32, shape, dim)


def divide(x, by):
    return ((x.astype(F32) + 0.5) * (1.0 / by)).astype(jnp.int32)


def dot(a, b, contract):
    return lax.dot_general(a, b, (contract, ((), ())), preferred_element_type=F32)


def expert_of(peer, z):
    return (peer >> 2) * 32 + z * 4 + (peer & 3)


def row_keys(rows, lanes):
    index = iota((NEAR * rows, lanes), 0)
    source = divide(index, rows)
    return (source * 16 + index - source * rows).astype(F32)


def pack_kernel(rows, ready, place_ref, *refs):
    blocks = refs[:NEAR]
    early = refs[NEAR : NEAR + ready]
    outs = refs[NEAR + ready : NEAR + ready + PEERS]
    key_ref, whi_ref, wlo_ref, tok, side, mask = refs[NEAR + ready + PEERS :]
    toks = blocks[0].shape[0]
    wide = tok.shape[1]
    experts = key_ref.shape[0]
    me, z = place_ref[0], place_ref[1]
    before, after = iota((toks, toks), 0), iota((toks, toks), 1)
    same = before == after
    tally = jnp.where(same, 64.0, jnp.where(before < after, 1.0, 0.0)).astype(BF16)
    same = same.astype(BF16)
    eids = iota((toks, experts), 1).astype(F32)
    for o, block in enumerate(blocks):
        side[o] = block[:, wide : wide + 128].astype(F32)
        tok[o * toks : (o + 1) * toks, :] = block[:, :wide]

    def route(pair, _):
        keys, highs, lows = [], [], []
        for n in range(2):
            lanes = side[pair * 2 + n]
            named = jnp.zeros((toks, experts), F32)
            high = jnp.zeros((toks, experts), F32)
            low = jnp.zeros((toks, experts), F32)
            for k in range(TOP):
                hit = lanes[:, k : k + 1] == eids
                named = named + jnp.where(hit, 1.0, 0.0)
                high = high + jnp.where(hit, lanes[:, TOP + k : TOP + k + 1], 0.0)
                low = low + jnp.where(hit, lanes[:, 2 * TOP + k : 2 * TOP + k + 1], 0.0)
            rank = dot(named.astype(BF16), tally, ((0,), (0,))) - 64.0
            first = (16 * (pair * 2 + n)).astype(F32)
            keys.append(jnp.where((rank > -0.5) & (rank < rows), rank + first, -1.0))
            highs.append(dot(high.astype(BF16), same, ((0,), (0,))))
            lows.append(dot(low.astype(BF16), same, ((0,), (0,))))
        here = pl.ds(pl.multiple_of(pair * 2 * toks, 2 * toks), 2 * toks)
        key_ref[:, here] = jnp.concatenate(keys, axis=1)
        whi_ref[:, here] = jnp.concatenate(highs, axis=1)
        wlo_ref[:, here] = jnp.concatenate(lows, axis=1)
        return 0

    lax.fori_loop(0, NEAR // 2, route, 0)
    part = NEAR * rows
    keys = row_keys(rows, NEAR * toks)

    def fill(m, _):
        row = key_ref[pl.ds(expert_of(me ^ m, z), 1), :]
        to = pl.ds(pl.multiple_of(m * part, part), part)
        mask[to, :] = jnp.where(row == keys, 1.0, 0.0).astype(BF16)
        return 0

    lax.fori_loop(0, PEERS, fill, 0)

    def columns(c, _):
        here = pl.ds(pl.multiple_of(c * 512, 512), 512)
        y = dot(mask[...], tok[:, here], ((1,), (0,)))
        for m, out in enumerate(outs):
            out[:part, here] = y[m * part : (m + 1) * part, :].astype(BF16)
        return 0

    lax.fori_loop(0, wide // 512, columns, 0)
    for out, ref in zip(outs, early):
        out[part:, :] = ref[...]


def pack(place, blocks, early, wide, experts, rows):
    toks = blocks[0].shape[0]
    groups = 2 if early else 1
    shape = jax.ShapeDtypeStruct((groups * NEAR * rows, wide), BF16)
    small = jax.ShapeDtypeStruct((experts, NEAR * toks), F32)
    vm = pl.BlockSpec(memory_space=pltpu.VMEM)
    return pl.pallas_call(
        functools.partial(pack_kernel, rows, len(early)),
        in_specs=[pl.BlockSpec(memory_space=pltpu.SMEM)] + [vm] * (NEAR + len(early)),
        out_specs=[vm] * (PEERS + 3),
        out_shape=[shape] * PEERS + [small] * 3,
        scratch_shapes=[
            pltpu.VMEM((NEAR * toks, wide), BF16),
            pltpu.VMEM((NEAR, toks, 128), F32),
            pltpu.VMEM((PEERS * NEAR * rows, NEAR * toks), BF16),
        ],
        name="pack",
    )(place, *blocks, *early)


def weigh_kernel(rows, place_ref, key_ref, whi_ref, wlo_ref, ret_ref, *refs):
    *outs, left = refs
    z = place_ref[1]
    span = key_ref.shape[1]
    toks = outs[0].shape[0]
    keys = row_keys(rows, span)
    part = keys.shape[0]

    def fill(j, _):
        e = expert_of(j, z)
        to = pl.ds(pl.multiple_of(j * part, part), part)
        hit = key_ref[pl.ds(e, 1), :] == keys
        left[to, :span] = jnp.where(hit, whi_ref[pl.ds(e, 1), :], 0.0).astype(BF16)
        left[to, span:] = jnp.where(hit, wlo_ref[pl.ds(e, 1), :], 0.0).astype(BF16)
        return 0

    lax.fori_loop(0, PEERS, fill, 0)

    def columns(c, _):
        here = pl.ds(pl.multiple_of(c * 512, 512), 512)
        y = dot(left[...], ret_ref[:, here], ((0,), (0,)))
        y = y[:span] + y[span:]
        for o, out in enumerate(outs):
            out[:, here] = y[o * toks : (o + 1) * toks, :].astype(out.dtype)
        return 0

    lax.fori_loop(0, ret_ref.shape[1] // 512, columns, 0)


def weigh(place, keys, whi, wlo, ret, rows, kinds):
    _, lanes = keys.shape
    toks = lanes // NEAR
    wide = ret.shape[1]
    vm = pl.BlockSpec(memory_space=pltpu.VMEM)
    return pl.pallas_call(
        functools.partial(weigh_kernel, rows),
        in_specs=[pl.BlockSpec(memory_space=pltpu.SMEM)] + [vm] * 4,
        out_specs=[vm] * NEAR,
        out_shape=[jax.ShapeDtypeStruct((toks, wide), kind) for kind in kinds],
        scratch_shapes=[pltpu.VMEM((ret.shape[0], 2 * lanes), BF16)],
        name="weigh",
    )(place, keys, whi, wlo, ret)


def expert_kernel(place_ref, *refs):
    xin = refs[:PEERS]
    g0, u0, d0, g1, u1, d1, g2, u2, d2 = refs[PEERS : PEERS + 9]
    o_ref, wg, wu, wd, xs, acc, sems = refs[PEERS + 9 :]
    half = g0.shape[0]
    quarter = g1.shape[0]
    copies = []
    for i, (src, dst, start) in enumerate(
        [
            (g0, wg, 0),
            (u0, wu, 0),
            (d0, wd, 0),
            (g1, wg, half),
            (u1, wu, half),
            (g2, wg, half + quarter),
            (u2, wu, half + quarter),
            (d1, wd, half),
            (d2, wd, half + quarter),
        ]
    ):
        copy = pltpu.make_async_copy(src, dst.at[pl.ds(start, src.shape[0])], sems.at[i])
        copy.start()
        copies.append(copy)

    part = xin[0].shape[0]
    for m in range(PEERS):
        xs[m * part : (m + 1) * part, :] = xin[m][...]

    me = place_ref[0]

    def clear(m, _):
        here = pl.ds(pl.multiple_of(m * part, part), part)
        acc[here, :] = jnp.zeros((part, acc.shape[1]), F32)
        return 0

    lax.fori_loop(0, PEERS, clear, 0)
    for copy in copies[:3]:
        copy.wait()

    def run(n, _):
        @pl.when(n == 1)
        def _():
            for copy in copies[3:]:
                copy.wait()

        here = pl.ds(pl.multiple_of(n * half, half), half)
        x = xs[...]
        gate = dot(x, wg[here, :], ((1,), (1,)))
        upper = dot(x, wu[here, :], ((1,), (1,)))
        hidden = (gate / (1.0 + jnp.exp(-gate)) * upper).astype(BF16)
        acc[...] = acc[...] + dot(hidden, wd[here, :], ((1,), (0,)))
        return 0

    lax.fori_loop(0, 2, run, 0)

    def leave(m, _):
        o_ref[me ^ m] = acc[pl.ds(pl.multiple_of(m * part, part), part), :].astype(BF16)
        return 0

    lax.fori_loop(0, PEERS, leave, 0)


def expert(place, x, own, first, second, group, rows):
    half, wide = own[0].shape
    total = 2 * half
    part = NEAR * rows
    count = PEERS * part
    anyspec = pl.BlockSpec(memory_space=pl.ANY)
    return pl.pallas_call(
        expert_kernel,
        grid=(1,),
        in_specs=[pl.BlockSpec(memory_space=pltpu.SMEM)]
        + [pl.BlockSpec((part, wide), lambda i: (group, 0))] * PEERS
        + [anyspec] * 9,
        out_specs=pl.BlockSpec((PEERS, part, wide), lambda i: (0, 0, 0)),
        out_shape=jax.ShapeDtypeStruct((PEERS, part, wide), BF16),
        scratch_shapes=[
            pltpu.VMEM((total, wide), BF16),
            pltpu.VMEM((total, wide), BF16),
            pltpu.VMEM((total, wide), BF16),
            pltpu.VMEM((count, wide), BF16),
            pltpu.VMEM((count, wide), F32),
            pltpu.SemaphoreType.DMA((9,)),
        ],
        compiler_params=pltpu.CompilerParams(vmem_limit_bytes=60 * 1024 * 1024),
        cost_estimate=pl.CostEstimate(
            flops=6 * count * total * wide,
            bytes_accessed=6 * total * wide + 4 * count * wide,
            transcendentals=count * total,
        ),
        name="expert",
    )(place, *x, *own, *first, *second)


def leave_kernel(place_ref, table_ref, in_ref, same_ref, first_ref, later_ref, used):
    z, x, column = place_ref[1], place_ref[2], place_ref[3]
    blk_dev = in_ref.shape[1]

    def clear(p, _):
        used[p] = 0
        return 0

    lax.fori_loop(0, 2 * ZS, clear, 0)

    def one(i, _):
        dest = table_ref[column, (x * ZS + z) * blk_dev + i] // blk_dev
        rank = used[dest]
        used[dest] = rank + 1
        far = dest & (ZS - 1)

        @pl.when(dest // ZS == x)
        def _():
            same_ref[far, rank] = in_ref[:, i]

        @pl.when((dest // ZS != x) & (rank == 0))
        def _():
            first_ref[(far - z) & (ZS - 1)] = in_ref[:, i]

        @pl.when((dest // ZS != x) & (rank == 1))
        def _():
            later_ref[(far - z) & (ZS - 1)] = in_ref[:, i]

        return 0

    lax.fori_loop(0, blk_dev, one, 0)


def gather_out(place, table, cache, spare):
    layers, _, blk, wide = cache.shape
    smem = pl.BlockSpec(memory_space=pltpu.SMEM)
    vm = pl.BlockSpec(memory_space=pltpu.VMEM)
    shape = jax.ShapeDtypeStruct((ZS, spare, layers, blk, wide), cache.dtype)
    single = jax.ShapeDtypeStruct((ZS, layers, blk, wide), cache.dtype)
    return pl.pallas_call(
        leave_kernel,
        in_specs=[smem, smem, vm],
        out_specs=[vm, vm, vm],
        out_shape=[shape, single, single],
        scratch_shapes=[pltpu.SMEM((2 * ZS,), jnp.int32)],
        name="gather_out",
    )(place, table, cache)


def join_kernel(first_ref, later_ref, *outs):
    for n, out in enumerate(outs):
        out[0] = first_ref[n + 1]
        out[1] = later_ref[n + 1]


def join(first, later):
    vm = pl.BlockSpec(memory_space=pltpu.VMEM)
    return pl.pallas_call(
        join_kernel,
        in_specs=[vm] * 2,
        out_specs=[vm] * (ZS - 1),
        out_shape=[jax.ShapeDtypeStruct((2,) + first.shape[1:], first.dtype)] * (ZS - 1),
        name="join",
    )(first, later)


def collect_kernel(later_ref, *refs):
    out = refs[-1]
    out[0] = later_ref[0]
    for n, ref in enumerate(refs[:-1]):
        out[n + 1] = ref[1]


def collect(later, moved):
    vm = pl.BlockSpec(memory_space=pltpu.VMEM)
    return pl.pallas_call(
        collect_kernel,
        in_specs=[vm] * ZS,
        out_specs=vm,
        out_shape=jax.ShapeDtypeStruct(later.shape, later.dtype),
        name="collect",
    )(later, *moved)


def arrive_kernel(place_ref, slot_ref, same_ref, *refs):
    crossed, beyond_ref, out_ref = refs[:ZS], refs[ZS], refs[ZS + 1]
    z, x = place_ref[1], place_ref[2]
    spare = same_ref.shape[1]

    def put(source, i, ref):
        to = slot_ref[source * spare + i]

        @pl.when(to >= 0)
        def _():
            out_ref[:, to] = ref[...]

    def one(n, _):
        for i in range(spare):
            put(x * ZS + n, i, same_ref.at[n, i])
        return 0

    lax.fori_loop(0, ZS, one, 0)
    for n in range(ZS):
        put((1 - x) * ZS + ((z - n) & (ZS - 1)), 0, crossed[n].at[0])
        put((1 - x) * ZS + ((z - n) & (ZS - 1)), 1, beyond_ref.at[n])


def gather_in(place, slots, same, crossed, beyond, blk_dev):
    _, _, layers, blk, wide = same.shape
    smem = pl.BlockSpec(memory_space=pltpu.SMEM)
    vm = pl.BlockSpec(memory_space=pltpu.VMEM)
    return pl.pallas_call(
        arrive_kernel,
        in_specs=[smem, smem] + [vm] * (ZS + 2),
        out_specs=vm,
        out_shape=jax.ShapeDtypeStruct((layers, blk_dev, blk, wide), same.dtype),
        name="gather_in",
    )(place, slots, same, *crossed, beyond)


def arrival_slots(handover_table, sources, blk_dev, spare):
    column = lax.dynamic_index_in_dim(handover_table, lax.axis_index("tp"), 0, keepdims=False)
    here = lax.axis_index("pre")
    table = column.reshape(sources, blk_dev)
    dest = table // blk_dev
    earlier = jnp.arange(blk_dev)[:, None] < jnp.arange(blk_dev)[None, :]
    same = dest[:, :, None] == dest[:, None, :]
    rank = jnp.sum((same & earlier[None]).astype(jnp.int32), axis=1)
    wanted = jnp.arange(sources * spare, dtype=jnp.int32)
    came = jnp.arange(sources, dtype=jnp.int32)[:, None] * spare + rank
    came = jnp.where(dest == here, came, -1).reshape(-1)
    slots = jnp.where(wanted[:, None] == came[None, :], (column % blk_dev + 1)[None, :], 0)
    return jnp.sum(slots, axis=1) - 1


def shards(
    tokens,
    route_ids,
    route_weights,
    gate_weight,
    up_weight,
    down_weight,
    prefill_cache,
    handover_table,
):
    tok_dev, wide = tokens.shape
    top_count = route_ids.shape[1]
    tp = lax.axis_size("tp")
    groups = lax.axis_size("pre") * tp
    experts_all = groups // 2
    rows = min(tok_dev, 2 * tok_dev * top_count // experts_all)

    half = down_weight.shape[0]
    quarter = half // 2
    core = lax.axis_index("dec")
    swap = [(i, i ^ 1) for i in range(tp)]
    first, second = [], []
    own = (gate_weight.T, up_weight.T, down_weight)
    for weight in own:
        piece = lax.dynamic_slice_in_dim(weight, core * quarter, quarter, 0)
        got = lax.ppermute(piece, "tp", swap)
        first.append(got)
        second.append(lax.ppermute(got, "dec", [(0, 1), (1, 0)]))

    pre = lax.axis_size("pre")
    high = route_weights.astype(BF16)
    low = (route_weights - high.astype(F32)).astype(BF16)
    lanes = jnp.concatenate([route_ids.astype(BF16), high, low], axis=1)
    lanes = jnp.pad(lanes, ((0, 0), (0, 128 - 3 * top_count)))
    block = jnp.concatenate([tokens, lanes], axis=1)
    up = [(i, i // ZS * ZS + (i + 1) % ZS) for i in range(pre)]
    down = [(j, i) for i, j in up]
    below, above = [block], [block]
    for n in range(4):
        below.append(lax.ppermute(below[-1], "pre", up))
        if n < 3:
            above.append(lax.ppermute(above[-1], "pre", down))
    blocks = [below[4], below[3], above[3], below[2], above[2], below[1], above[1], block]

    here = lax.axis_index("pre")
    there = lax.axis_index("tp")
    me = (here // ZS) * 4 + there // 2
    place = jnp.stack([me, here % ZS, here // ZS, there]).astype(jnp.int32)
    *packed, keys, whi, wlo = pack(place, blocks[NEAR:], [], wide, experts_all, rows)
    routes = [(keys, whi, wlo)]
    *packed, keys, whi, wlo = pack(place, blocks[:NEAR], packed, wide, experts_all, rows)
    routes.insert(0, (keys, whi, wlo))

    def kind_of(group):
        return (group ^ (group >> 1)) & 1

    def peer_of(group, flip):
        p, t = group // tp, group % tp
        peer = ((p // ZS) * 4 + t // 2) ^ flip
        last = peer & 1
        return ((peer >> 2) * ZS + p % ZS) * tp + (peer & 2) * 2 + last * 2 + (last ^ kind_of(t))

    came = [packed[0]]
    for m in range(1, PEERS):
        came.append(
            lax.ppermute(packed[m], ("pre", "tp"), [(g, peer_of(g, m)) for g in range(groups)])
        )

    planes = [
        [g for g in range(groups) if g // tp % ZS == z and kind_of(g) == kind]
        for z in range(ZS)
        for kind in (0, 1)
    ]
    sums = []
    results = []
    for group in range(ZS // NEAR):
        results.append(expert(place, came, own, first, second, group, rows))
    for group, result in enumerate(results):
        back = lax.all_to_all(
            result,
            ("pre", "tp"),
            split_axis=0,
            concat_axis=0,
            axis_index_groups=planes,
            tiled=True,
        )
        kinds = (BF16, BF16, F32, F32) if group == 0 else (F32,) * NEAR
        sums += weigh(place, *routes[group], back.reshape(-1, wide), rows, kinds)

    rising, falling = sums[0], sums[1]
    for local in (sums[2], sums[4], sums[6], None):
        rising = lax.ppermute(rising, "pre", up)
        if local is not None:
            rising = (rising.astype(F32) + local).astype(BF16)
    for local in (sums[3], sums[5], None):
        falling = lax.ppermute(falling, "pre", down)
        if local is not None:
            falling = (falling.astype(F32) + local).astype(BF16)
    moe_output = (rising.astype(F32) + falling.astype(F32) + sums[7]).astype(BF16)

    _, _, blk_dev, _, _ = prefill_cache.shape
    sources = lax.axis_size("pre")
    spare = blk_dev // sources + 1
    in_slots = arrival_slots(handover_table, sources, blk_dev, spare)
    same, first_cross, later = gather_out(place, handover_table, prefill_cache[:, 0], spare)
    across = [(i, (i + ZS) % sources) for i in range(sources)]
    first_cross = lax.ppermute(first_cross, "pre", across)
    same = lax.all_to_all(
        same,
        "pre",
        split_axis=0,
        concat_axis=0,
        axis_index_groups=[list(range(x * ZS, (x + 1) * ZS)) for x in range(sources // ZS)],
        tiled=True,
    )
    crossed = []
    for n, both in enumerate(join(first_cross, later)):
        crossed.append(
            lax.ppermute(
                both, "pre", [(i, i // ZS * ZS + (i + n + 1) % ZS) for i in range(sources)]
            )
        )
    rest = collect(later, crossed)
    crossed = [first_cross] + crossed
    rest = lax.ppermute(rest, "pre", across)
    decode_cache = gather_in(place, in_slots, same, crossed, rest, blk_dev)[:, None]
    return (moe_output, decode_cache)


def solution(mesh):
    return jax.shard_map(
        shards,
        mesh=mesh,
        in_specs=(
            P(("pre", "tp", "dec"), None),
            P(("pre", "tp", "dec"), None),
            P(("pre", "tp", "dec"), None),
            P(None, ("pre", "tp")),
            P(None, ("pre", "tp")),
            P(("pre", "tp"), None),
            P(None, "tp", "pre", None, "dec"),
            P(),
        ),
        out_specs=(P(("pre", "tp", "dec"), None), P(None, "tp", "pre", None, "dec")),
        check_vma=False,
    )
```
